128 devices in a mesh: ax: 16 (over x, z), rad: 8 (over y, core).
Axes of the slice: x: 4, y: 4, z: 4, core: 2. Of those that a mesh axis runs over, the one named last changes fastest.
Arguments:
- forcing: float32 [32, 5, 256, 1024], P(None, None, 'ax', 'rad'), may hold values from -300 to 300, as said below
- vel_axial: float32 [256, 1024], P('ax', 'rad'), may hold values from 0.2 to 1
- vel_radial: float32 [256, 1024], P('ax', 'rad'), may hold values from -0.4 to 0.4
- coupling: float32 [5, 5, 256, 1024], P(None, None, 'ax', 'rad'), may hold values from -1.5 to 1.5
- viscosity: float32 [5], replicated, may hold values from 0.03 to 0.18
Outputs:
- basis: float32 [32, 5, 256, 1024], P(None, None, 'ax', 'rad')
- r_factor: float32 [32, 32], replicated
The draws below stay inside these ranges and needn't reach their ends.
Inputs may be any that keep to these rules, and one draw needn't show every extreme that they name: `forcing`: forcing of the linearized equations.
All inputs are finite; a program needn't handle non-finite values.
Results may differ from the reference program's by a relative error of at most 0.00024.
Values sent between devices are 32-bit elements; how exact they have to be, the bound alone decides.
No kernel may reach another device: no remote copies, remote signals or barrier semaphores. Data moves between devices by JAX's collectives and lax.ppermute only.
A program may use at most 64 MiB of HBM per device.

```python
import math
import jax
import jax.numpy as jnp
from jax import lax

K = 32
V = 5
STEPS = 3
NA = 256
NR = 1024
ROWS = 1310720


def draw_forcing(key, part):
    keys = jax.random.split(key, 4)
    axial = jnp.arange(NA, dtype=jnp.float32) / (NA - 1)
    own = jnp.clip(jax.random.normal(keys[0], (K, V, NA, NR), jnp.float32), -5.0, 5.0)
    common = jnp.clip(jax.random.normal(keys[1], (V, NA, NR), jnp.float32), -5.0, 5.0)
    weights = jax.random.uniform(keys[2], (K,), jnp.float32, 0.4, 0.8)
    envelope = 1.0 + 2.0 * axial
    scales = 10.0 ** jax.random.uniform(keys[3], (K,), jnp.float32, 0.0, 1.0)
    field = (own + weights[:, None, None, None] * common[None]) * envelope[None, None, :, None]
    field = field * scales[:, None, None, None]
    return field.astype(jnp.float32)


def block_levels(key, extent, pieces, least, high):
    def one(dim, shards_of):
        heights = jax.random.uniform(jax.random.fold_in(jax.random.fold_in(key, 6), dim), (shards_of,), jnp.float32, least / len(pieces), high / len(pieces))
        return jnp.repeat(jnp.exp(heights), extent[dim] // shards_of).reshape((-1,) + (1,) * (len(extent) - dim - 1))

    loudness = one(*pieces[0])
    for cut in pieces[1:]:
        loudness = loudness * one(*cut)
    return loudness


def centred(key, dims, deviation, limit, cuts=(), kind=jnp.bfloat16):
    values = jax.random.normal(key, dims, jnp.float32) * deviation
    if len(cuts) > 0:
        values = block_levels(key, dims, cuts, -0.22, 0.18) * values
    return jnp.clip(values, min=-limit, max=limit).astype(kind)


def setup_inputs(seed: int = 0) -> dict:
    arg_keys = jax.random.split(jax.random.key(seed), 6)
    forcing = draw_forcing(jax.random.fold_in(arg_keys[5], 71), 0)
    vel_axial = jnp.clip(0.2 + 0.8 * jax.random.uniform(arg_keys[1], (NA, NR), jnp.float32) ** block_levels(arg_keys[1], (NA, NR), ((0, 16), (1, 8)), -0.2, 0.2), 0.2, 1.0)
    vel_radial = jnp.clip(jax.random.uniform(arg_keys[2], (NA, NR), jnp.float32, -0.4, 0.4) * block_levels(arg_keys[2], (NA, NR), ((0, 16), (1, 8)), -0.4, 0.0), -0.4, 0.4)
    coupling = centred(arg_keys[3], (V, V, NA, NR), 0.3, 1.5, ((2, 16), (3, 8)), jnp.float32)
    viscosity = jnp.clip(jnp.exp(jax.random.uniform(arg_keys[4], (V,), jnp.float32, math.log(0.03), math.log(0.18))), 0.03, 0.18)
    return dict(forcing=forcing, vel_axial=vel_axial, vel_radial=vel_radial, coupling=coupling, viscosity=viscosity)


time_step = 0.8

def operate(padded, vel_axial, vel_radial, coupling, viscosity):
    center = padded[..., 2:-2, 2:-2]
    axial_up = padded[..., 3:-1, 2:-2]
    axial_down = padded[..., 1:-3, 2:-2]
    axial_far_up = padded[..., 4:, 2:-2]
    axial_far_down = padded[..., :-4, 2:-2]
    radial_up = padded[..., 2:-2, 3:-1]
    radial_down = padded[..., 2:-2, 1:-3]
    radial_far_up = padded[..., 2:-2, 4:]
    radial_far_down = padded[..., 2:-2, :-4]
    first_axial = (8.0 * (axial_up - axial_down) - (axial_far_up - axial_far_down)) / 12.0
    first_radial = (8.0 * (radial_up - radial_down) - (radial_far_up - radial_far_down)) / 12.0
    second = (16.0 * (axial_up + axial_down + radial_up + radial_down) - (axial_far_up + axial_far_down + radial_far_up + radial_far_down) - 60.0 * center) / 12.0
    result = -vel_axial * first_axial - vel_radial * first_radial + viscosity[:, None, None] * second
    for source in range(coupling.shape[1]):
        result = result + coupling[:, source] * center[..., source:source + 1, :, :]
    return result

def upper_inverse(upper_factor):
    order = upper_factor.shape[0]
    identity = jnp.eye(order, dtype=jnp.float32)

    def one_row(count, inverse):
        row_index = order - 1 - count
        factor_row = lax.dynamic_slice_in_dim(upper_factor, row_index, 1, 0)
        unit_row = lax.dynamic_slice_in_dim(identity, row_index, 1, 0)
        pivot = jnp.sum(factor_row * unit_row)
        new_row = (unit_row - jnp.dot(factor_row, inverse, precision=lax.Precision.HIGHEST)) / pivot
        return lax.dynamic_update_slice_in_dim(inverse, new_row, row_index, 0)
    return lax.fori_loop(0, order, one_row, jnp.zeros((order, order), jnp.float32))

def reference(forcing, vel_axial, vel_radial, coupling, viscosity):

    def apply_operator(field):
        padded = jnp.pad(field, ((0, 0), (2, 2), (2, 2)))
        return operate(padded, vel_axial, vel_radial, coupling, viscosity)

    def advance(vector):
        field_now = vector
        for step_index in range(STEPS):
            slope_one = apply_operator(field_now)
            middle = field_now + time_step * slope_one
            slope_two = apply_operator(middle)
            field_now = field_now + 0.5 * time_step * (slope_one + slope_two)
        return field_now
    response = lax.map(advance, forcing)
    flattened = response.reshape(K, ROWS)
    gram = jnp.dot(flattened, flattened.T, precision=lax.Precision.HIGHEST) / ROWS
    upper_factor = jnp.linalg.cholesky(gram).T
    inverse = upper_inverse(upper_factor)
    basis = jnp.dot(inverse.T, flattened, precision=lax.Precision.HIGHEST).reshape(response.shape)
    return (basis, upper_factor)
```

```python
import functools

import jax
import jax.numpy as jnp
from jax import lax
from jax.experimental import pallas as pl
from jax.experimental.pallas import tpu as pltpu
from jax.sharding import PartitionSpec as P

STEPS = 3


time_step = 0.8


def padded_2(shard, sides, width):
    for axis, dim in sides:
        size, length = (lax.axis_size(axis), shard.shape[dim])
        up = [(i, (i + 1) % size) for i in range(size - 1)]
        down = [(j, i) for i, j in up]
        last = lax.slice_in_dim(shard, length - width, length, axis=dim)
        initial = lax.slice_in_dim(shard, 0, width, axis=dim)
        before = lax.ppermute(last, axis, up)
        after = lax.ppermute(initial, axis, down)
        shard = jnp.concatenate([before, shard, after], axis=dim)
    return shard


def operate(padded, vel_axial, vel_radial, coupling, viscosity):
    center = padded[..., 2:-2, 2:-2]
    axial_up = padded[..., 3:-1, 2:-2]
    axial_down = padded[..., 1:-3, 2:-2]
    axial_far_up = padded[..., 4:, 2:-2]
    axial_far_down = padded[..., :-4, 2:-2]
    radial_up = padded[..., 2:-2, 3:-1]
    radial_down = padded[..., 2:-2, 1:-3]
    radial_far_up = padded[..., 2:-2, 4:]
    radial_far_down = padded[..., 2:-2, :-4]
    first_axial = (8.0 * (axial_up - axial_down) - (axial_far_up - axial_far_down)) / 12.0
    first_radial = (8.0 * (radial_up - radial_down) - (radial_far_up - radial_far_down)) / 12.0
    second = (
        16.0 * (axial_up + axial_down + radial_up + radial_down)
        - (axial_far_up + axial_far_down + radial_far_up + radial_far_down)
        - 60.0 * center
    ) / 12.0
    result = (
        -vel_axial * first_axial - vel_radial * first_radial + viscosity[:, None, None] * second
    )
    for source in range(coupling.shape[1]):
        result = result + coupling[:, source] * center[..., source : source + 1, :, :]
    return result


def factor_kernel(parts_ref, factor_ref, inverse_ref, *, rows_all):
    total = jnp.sum(parts_ref[...], axis=0) * (1.0 / rows_all)
    order = factor_ref.shape[0]
    lane = lax.broadcasted_iota(jnp.int32, (order, 128), 1)
    row = lax.broadcasted_iota(jnp.int32, (order, 128), 0)
    pieces = [total] + [pltpu.roll(total, 128 - 32 * i, axis=1) for i in range(1, 4)]
    work = jnp.concatenate(pieces, axis=0)
    work = jnp.where(lane < order, work, jnp.where(lane == row + order, 1.0, 0.0))
    for j in range(order - 1):
        pivot_row = work[j : j + 1, :]
        scale = pivot_row / pivot_row[:, j : j + 1]
        column = jnp.where(row > j, jnp.broadcast_to(work[:, j : j + 1], work.shape), 0.0)
        work = work - column * scale
    diagonal = jnp.sum(jnp.where(lane == row, work, 0.0), axis=1, keepdims=True)
    work = work / jnp.sqrt(diagonal)
    factor_ref[...] = jnp.where(lane >= row, work, 0.0)[:, :order]
    inverse_ref[...] = jnp.where(lane <= row, pltpu.roll(work, 128 - order, axis=1), 0.0)[:, :order]


def factor_and_inverse(parts, order, rows_all):
    square = jax.ShapeDtypeStruct((order, order), jnp.float32)
    return pl.pallas_call(
        functools.partial(factor_kernel, rows_all=rows_all),
        out_shape=(square, square),
        name="factor",
    )(parts)


def rim_operator(field_now, vel_axial, vel_radial, coupling, viscosity):
    padded = padded_2(field_now, (("ax", 2), ("rad", 3)), 2)
    return operate(padded, vel_axial, vel_radial, coupling, viscosity)


def per_device(forcing, vel_axial, vel_radial, coupling, viscosity):
    vectors, variables, axial_cells, radial_cells = forcing.shape
    field_now = forcing
    for step_index in range(STEPS):
        slope_one = rim_operator(field_now, vel_axial, vel_radial, coupling, viscosity)
        middle = field_now + time_step * slope_one
        slope_two = rim_operator(middle, vel_axial, vel_radial, coupling, viscosity)
        field_now = field_now + 0.5 * time_step * (slope_one + slope_two)
    flattened = field_now.reshape(vectors, variables * axial_cells * radial_cells)
    rows_all = variables * axial_cells * radial_cells * lax.axis_size("ax") * lax.axis_size("rad")
    local_gram = jnp.dot(flattened, flattened.T, precision=lax.Precision.HIGHEST)
    packed = jnp.concatenate([local_gram[8 * i : 8 * i + 8] for i in range(4)], axis=1)
    devices = lax.axis_size("ax") * lax.axis_size("rad")
    copies = jnp.broadcast_to(packed, (devices, 8, 128))
    parts = lax.all_to_all(copies, ("ax", "rad"), 0, 0)
    upper_factor, lower_inverse = factor_and_inverse(parts, vectors, rows_all)
    basis = jnp.dot(lower_inverse, flattened, precision=lax.Precision.HIGHEST).reshape(field_now.shape)
    return (basis, upper_factor)


def solution(mesh):
    return jax.shard_map(
        per_device,
        mesh=mesh,
        in_specs=(
            P(None, None, "ax", "rad"),
            P("ax", "rad"),
            P("ax", "rad"),
            P(None, None, "ax", "rad"),
            P(),
        ),
        out_specs=(P(None, None, "ax", "rad"), P()),
        check_vma=False,
    )
```

```python
import functools

import jax
import jax.numpy as jnp
from jax import lax
from jax.experimental import pallas as pl
from jax.experimental.pallas import tpu as pltpu
from jax.sharding import PartitionSpec as P

STEPS = 3
TIME_STEP = 0.8
SECTIONS = 2 * STEPS
WIDTH = 2 * SECTIONS
V = 5
GROUP = 16
PER = 128 // GROUP
PLANES = V * V + 3
WEIGHTS = V * (V + 8)
VMEM_LIMIT = 56 << 20


def whole(count):
    return [pl.BlockSpec(memory_space=pltpu.VMEM) for _ in range(count)]


def lanes_of(shape):
    return lax.broadcasted_iota(jnp.int32, shape, 1)


def pack_axial_kernel(field_ref, coupling_ref, axial_ref, radial_ref, up_ref, down_ref):
    planes, length, _ = field_ref.shape
    low = length - WIDTH

    def put(slot, read):
        base = slot * WIDTH
        for start in range(0, WIDTH, 8):
            size = min(8, WIDTH - start)
            up_ref[pl.ds(base + start, size), :] = read(low + start, size)
            down_ref[pl.ds(base + start, size), :] = read(start, size)

    @pl.loop(0, planes // 8)
    def _(block):
        for inner in range(8):
            plane = block * 8 + inner
            put(plane, lambda start, size: field_ref[plane, pl.ds(start, size), :])

    for plane in range(V * V):
        put(planes + plane, lambda start, size: coupling_ref[plane, pl.ds(start, size), :])
    put(planes + V * V, lambda start, size: axial_ref[pl.ds(start, size), :])
    put(planes + V * V + 1, lambda start, size: radial_ref[pl.ds(start, size), :])
    put(planes + V * V + 2, lambda start, size: jnp.ones((size, 128), jnp.float32))


def chunks(length):
    rim = sorted({*range(0, WIDTH - 7, 8), WIDTH - 8})
    return (
        [(0, row, row) for row in rim]
        + [(1, row, WIDTH + row) for row in range(0, length, 8)]
        + [(2, row, WIDTH + length + row) for row in rim]
    )


def coefficient(plane, source, row, planes, coupling_ref, axial_ref, radial_ref, low_ref, high_ref):
    if source != 1:
        ref = low_ref if source == 0 else high_ref
        return ref[pl.ds((planes + plane) * WIDTH + row, 8), :]
    if plane < V * V:
        return coupling_ref[plane, pl.ds(row, 8), :]
    if plane == V * V + 2:
        return jnp.ones((8, 128), jnp.float32)
    return (axial_ref if plane == V * V else radial_ref)[pl.ds(row, 8), :]


def pack_radial_kernel(
    field_ref, coupling_ref, axial_ref, radial_ref, low_ref, high_ref, right_ref, left_ref
):
    planes, length, _ = field_ref.shape
    groups = planes // (V * PER)
    lane = lanes_of((8, 128))

    def merge(tiles, offset):
        merged = pltpu.roll(tiles[0], offset, axis=1)
        for j in range(1, len(tiles)):
            merged = jnp.where(
                lane >= GROUP * j, pltpu.roll(tiles[j], (GROUP * j + offset) % 128, axis=1), merged
            )
        return merged

    def put(slot, row, tiles):
        right_ref[slot, pl.ds(row, 8), :] = merge(tiles, WIDTH)
        left_ref[slot, pl.ds(row, 8), :] = merge(tiles, 2)

    @pl.loop(0, groups * V)
    def _(slot):
        group, v = slot // V, slot % V
        for source, row, target in chunks(length):
            tiles = []
            for j in range(PER):
                plane = (group * PER + j) * V + v
                if source == 1:
                    tiles.append(field_ref[plane, pl.ds(row, 8), :])
                else:
                    ref = low_ref if source == 0 else high_ref
                    tiles.append(ref[pl.ds(plane * WIDTH + row, 8), :])
            put(slot, target, tiles)

    for slot in range(-(-PLANES // PER)):
        for source, row, target in chunks(length):
            tiles = [
                coefficient(
                    plane, source, row, planes, coupling_ref, axial_ref, radial_ref, low_ref, high_ref
                )
                for plane in range(slot * PER, min(PLANES, (slot + 1) * PER))
            ]
            put(groups * V + slot, target, tiles)


def weights_of(raw, viscosity):
    axial = raw[V * V] * (-TIME_STEP / 12.0)
    radial = raw[V * V + 1] * (-TIME_STEP / 12.0)
    inside = raw[V * V + 2]
    found = []
    for v in range(V):
        spread = inside * (viscosity[v] * (TIME_STEP / 12.0))
        for w in range(V):
            value = raw[v * V + w] * TIME_STEP
            found.append(value + (1.0 - 60.0 * spread) if v == w else value)
        for speed in (axial, radial):
            found.append(16.0 * spread + 8.0 * speed)
            found.append(16.0 * spread - 8.0 * speed)
            found.append(-spread - speed)
            found.append(speed - spread)
    return found


def steps_kernel(
    viscosity_ref,
    field_ref,
    coupling_ref,
    axial_ref,
    radial_ref,
    low_ref,
    high_ref,
    left_ref,
    right_ref,
    out_ref,
    now_ref,
    middle_ref,
    now_rim_ref,
    middle_rim_ref,
    weight_ref,
):
    planes, length, _ = field_ref.shape
    vectors = planes // V
    groups = vectors // PER
    slots = groups * V
    extended = length + 2 * WIDTH
    lane = lanes_of((8, 128))
    place = lane % GROUP
    viscosity = [viscosity_ref[v] for v in range(V)]

    @pl.loop(0, planes // 8)
    def _(block):
        for inner in range(8):
            plane = block * 8 + inner
            for source, row, target in chunks(length):
                if source == 1:
                    value = field_ref[plane, pl.ds(row, 8), :]
                else:
                    ref = low_ref if source == 0 else high_ref
                    value = ref[pl.ds(plane * WIDTH + row, 8), :]
                now_ref[plane, pl.ds(target, 8), :] = value

    @pl.loop(0, slots)
    def _(slot):
        for row in range(0, extended, 8):
            now_rim_ref[0, slot, pl.ds(row, 8), :] = left_ref[slot, pl.ds(row, 8), :]
            now_rim_ref[1, slot, pl.ds(row, 8), :] = right_ref[slot, pl.ds(row, 8), :]

    for source, row, target in chunks(length):
        raw = [
            coefficient(
                plane, source, row, planes, coupling_ref, axial_ref, radial_ref, low_ref, high_ref
            )
            for plane in range(PLANES)
        ]
        for index, value in enumerate(weights_of(raw, viscosity)):
            weight_ref[0, index, pl.ds(target, 8), :] = value

    @pl.loop(0, extended // 8)
    def _(block):
        start = pl.multiple_of(block * 8, 8)
        for side, ref in ((0, left_ref), (1, right_ref)):
            raw = []
            for plane in range(PLANES):
                tile = ref[slots + plane // PER, pl.ds(start, 8), :]
                tile = pltpu.roll(tile, (128 - GROUP * (plane % PER)) % 128, axis=1)
                tile = jnp.where(lane < GROUP, tile, 0.0)
                reach = GROUP
                while reach < 128:
                    tile = tile + pltpu.roll(tile, reach, axis=1)
                    reach *= 2
                raw.append(tile)
            for index, value in enumerate(weights_of(raw, viscosity)):
                weight_ref[1 + side, index, pl.ds(start, 8), :] = value

    def euler(v, kind, start, count, centers, vertical, sideways):
        def weight(index):
            return weight_ref[kind, v * (V + 8) + index, pl.ds(start, 8), :]

        totals = None
        for w in range(V):
            factor = weight(w)
            terms = [factor * centers[i][w] for i in range(count)]
            totals = terms if totals is None else [a + b for a, b in zip(totals, terms)]
        for index, step in enumerate((1, -1, 2, -2)):
            factor = weight(V + index)
            totals = [totals[i] + factor * vertical(i, step) for i in range(count)]
        for index, step in enumerate((1, -1, 2, -2)):
            factor = weight(V + 4 + index)
            totals = [totals[i] + factor * sideways(i, step) for i in range(count)]
        return totals

    for section in range(1, SECTIONS + 1):
        odd = section % 2 == 1
        last = section == SECTIONS
        source, source_rim = (now_ref, now_rim_ref) if odd else (middle_ref, middle_rim_ref)
        target, target_rim = (middle_ref, middle_rim_ref) if odd else (now_ref, now_rim_ref)
        first = 2 * section
        blocks = -(-(extended - 2 * first) // 8)

        @pl.loop(0, groups * blocks)
        def _(index):
            group, block = index // blocks, index % blocks
            start = first + block * 8
            joints = []
            for v in range(V):
                slot = group * V + v
                own = None
                for j in range(PER):
                    tile = source[(group * PER + j) * V + v, pl.ds(start, 8), :]
                    tile = pltpu.roll(tile, (GROUP * j + WIDTH) % 128, axis=1)
                    own = tile if own is None else jnp.where(lane >= GROUP * j, tile, own)
                left = source_rim[0, slot, pl.ds(start, 8), :]
                right = source_rim[1, slot, pl.ds(start, 8), :]
                inner = (place == WIDTH) | (place == WIDTH + 1)
                joints.append(jnp.where(inner, pltpu.roll(right, WIDTH - 2, axis=1), left))
                if not last:
                    source_rim[0, slot, pl.ds(start, 8), :] = jnp.where(inner, own, left)
                    source_rim[1, slot, pl.ds(start, 8), :] = jnp.where(
                        place < 2, pltpu.roll(own, 128 - (WIDTH - 2), axis=1), right
                    )

            if not last:
                for side in range(2):
                    slot = group * V
                    centers = [
                        [source_rim[side, slot + w, pl.ds(start, 8), :] for w in range(V)]
                    ]
                    for v in range(V):
                        (value,) = euler(
                            v,
                            1 + side,
                            start,
                            1,
                            centers,
                            lambda i, step: source_rim[side, slot + v, pl.ds(start + step, 8), :],
                            lambda i, step: pltpu.roll(centers[0][v], (128 - step) % 128, axis=1),
                        )
                        if not odd:
                            value = 0.5 * (value + target_rim[side, slot + v, pl.ds(start, 8), :])
                        target_rim[side, slot + v, pl.ds(start, 8), :] = value

            @pl.loop(0, PER // TOGETHER)
            def _(part):
                bases = [(group * PER + part * TOGETHER + i) * V for i in range(TOGETHER)]
                centers = [
                    [source[base + w, pl.ds(start, 8), :] for w in range(V)] for base in bases
                ]
                for v in range(V):
                    rims = [
                        pltpu.roll(
                            joints[v],
                            256 - WIDTH - GROUP * (part * TOGETHER + i),
                            axis=1,
                        )
                        for i in range(TOGETHER)
                    ]
                    edges = {1: lane == 0, 2: lane <= 1, -1: lane == 127, -2: lane >= 126}

                    def sideways(i, step):
                        tile = jnp.where(edges[step], rims[i], centers[i][v])
                        return pltpu.roll(tile, (128 - step) % 128, axis=1)

                    values = euler(
                        v,
                        0,
                        start,
                        TOGETHER,
                        centers,
                        lambda i, step: source[bases[i] + v, pl.ds(start + step, 8), :],
                        sideways,
                    )
                    for i in range(TOGETHER):
                        value = values[i]
                        if not odd:
                            value = 0.5 * (value + target[bases[i] + v, pl.ds(start, 8), :])
                        if last:
                            out_ref[bases[i] + v, pl.ds(start - WIDTH, 8), :] = value
                        else:
                            target[bases[i] + v, pl.ds(start, 8), :] = value


TOGETHER = 2


def factor_kernel(parts_ref, factor_ref, inverse_ref, *, rows_all):
    total = jnp.sum(parts_ref[...], axis=0) * (1.0 / rows_all)
    order = factor_ref.shape[0]
    lane = lax.broadcasted_iota(jnp.int32, (order, 128), 1)
    row = lax.broadcasted_iota(jnp.int32, (order, 128), 0)
    pieces = [total] + [pltpu.roll(total, 128 - 32 * i, axis=1) for i in range(1, 4)]
    work = jnp.concatenate(pieces, axis=0)
    work = jnp.where(lane < order, work, jnp.where(lane == row + order, 1.0, 0.0))
    for j in range(order - 1):
        pivot_row = work[j : j + 1, :]
        scale = pivot_row / pivot_row[:, j : j + 1]
        column = jnp.where(row > j, jnp.broadcast_to(work[:, j : j + 1], work.shape), 0.0)
        work = work - column * scale
    diagonal = jnp.sum(jnp.where(lane == row, work, 0.0), axis=1, keepdims=True)
    work = work / jnp.sqrt(diagonal)
    factor_ref[...] = jnp.where(lane >= row, work, 0.0)[:, :order]
    inverse_ref[...] = jnp.where(lane <= row, pltpu.roll(work, 128 - order, axis=1), 0.0)[:, :order]


def factor_and_inverse(parts, order, rows_all):
    square = jax.ShapeDtypeStruct((order, order), jnp.float32)
    return pl.pallas_call(
        functools.partial(factor_kernel, rows_all=rows_all),
        out_shape=(square, square),
        name="factor",
    )(parts)


def shape_of(*dims):
    return jax.ShapeDtypeStruct(dims, jnp.float32)


def shifted(block, axis, step):
    size = lax.axis_size(axis)
    return lax.ppermute(
        block, axis, [(i, i + step) for i in range(size) if 0 <= i + step < size]
    )


def per_device(forcing, vel_axial, vel_radial, coupling, viscosity):
    vectors, variables, length, columns = forcing.shape
    planes = vectors * variables
    extended = length + 2 * WIDTH
    field = forcing.reshape(planes, length, columns)
    local = (field, coupling.reshape(V * V, length, columns), vel_axial, vel_radial)
    params = pltpu.CompilerParams(vmem_limit_bytes=VMEM_LIMIT)

    strip = shape_of((planes + PLANES) * WIDTH, columns)
    up, down = pl.pallas_call(
        pack_axial_kernel,
        in_specs=whole(4),
        out_specs=whole(2),
        out_shape=(strip, strip),
        compiler_params=params,
        name="pack_axial",
    )(*local)
    low = shifted(up, "ax", 1)
    high = shifted(down, "ax", -1)

    rim_slots = planes // PER + -(-PLANES // PER)
    rim = shape_of(rim_slots, extended, columns)
    to_right, to_left = pl.pallas_call(
        pack_radial_kernel,
        in_specs=whole(6),
        out_specs=whole(2),
        out_shape=(rim, rim),
        compiler_params=params,
        name="pack_radial",
    )(*local, low, high)
    left = shifted(to_right, "rad", 1)
    right = shifted(to_left, "rad", -1)

    rows = extended + 8
    response = pl.pallas_call(
        steps_kernel,
        in_specs=[pl.BlockSpec(memory_space=pltpu.SMEM)] + whole(8),
        out_specs=whole(1)[0],
        out_shape=shape_of(planes, length, columns),
        scratch_shapes=[
            pltpu.VMEM((planes, rows, columns), jnp.float32),
            pltpu.VMEM((planes, rows, columns), jnp.float32),
            pltpu.VMEM((2, planes // PER, rows, columns), jnp.float32),
            pltpu.VMEM((2, planes // PER, rows, columns), jnp.float32),
            pltpu.VMEM((3, WEIGHTS, rows, columns), jnp.float32),
        ],
        compiler_params=params,
        name="steps",
    )(viscosity, *local, low, high, left, right)

    flattened = response.reshape(vectors, variables * length * columns)
    devices = lax.axis_size("ax") * lax.axis_size("rad")
    rows_all = variables * length * columns * devices
    local_gram = jnp.dot(flattened, flattened.T, precision=lax.Precision.HIGHEST)
    packed = jnp.concatenate([local_gram[8 * i : 8 * i + 8] for i in range(4)], axis=1)
    copies = jnp.broadcast_to(packed, (devices, 8, 128))
    parts = lax.all_to_all(copies, ("ax", "rad"), 0, 0)
    upper_factor, lower_inverse = factor_and_inverse(parts, vectors, rows_all)
    basis = jnp.dot(lower_inverse, flattened, precision=lax.Precision.HIGHEST).reshape(forcing.shape)
    return (basis, upper_factor)


def solution(mesh):
    return jax.shard_map(
        per_device,
        mesh=mesh,
        in_specs=(
            P(None, None, "ax", "rad"),
            P("ax", "rad"),
            P("ax", "rad"),
            P(None, None, "ax", "rad"),
            P(),
        ),
        out_specs=(P(None, None, "ax", "rad"), P()),
        check_vma=False,
    )
```

```python
import functools

import jax
import jax.numpy as jnp
from jax import lax
from jax.experimental import pallas as pl
from jax.experimental.pallas import tpu as pltpu
from jax.sharding import PartitionSpec as P

STEPS = 3
TIME_STEP = 0.8
SECTIONS = 2 * STEPS
WIDTH = 2 * SECTIONS
V = 5
GROUP = 16
PER = 128 // GROUP
PLANES = V * V + 3
WEIGHTS = V * (V + 8)
VMEM_LIMIT = 56 << 20


def whole(count):
    return [pl.BlockSpec(memory_space=pltpu.VMEM) for _ in range(count)]


def lanes_of(shape):
    return lax.broadcasted_iota(jnp.int32, shape, 1)


def pack_axial_kernel(field_ref, coupling_ref, axial_ref, radial_ref, up_ref, down_ref):
    planes, length, _ = field_ref.shape
    low = length - WIDTH

    def put(slot, read):
        base = slot * WIDTH
        for start in range(0, WIDTH, 8):
            size = min(8, WIDTH - start)
            up_ref[pl.ds(base + start, size), :] = read(low + start, size)
            down_ref[pl.ds(base + start, size), :] = read(start, size)

    @pl.loop(0, planes // 8)
    def _(block):
        for inner in range(8):
            plane = block * 8 + inner
            put(plane, lambda start, size: field_ref[plane, pl.ds(start, size), :])

    for plane in range(V * V):
        put(planes + plane, lambda start, size: coupling_ref[plane, pl.ds(start, size), :])
    put(planes + V * V, lambda start, size: axial_ref[pl.ds(start, size), :])
    put(planes + V * V + 1, lambda start, size: radial_ref[pl.ds(start, size), :])
    put(planes + V * V + 2, lambda start, size: jnp.ones((size, 128), jnp.float32))


def chunks(length):
    rim = sorted({*range(0, WIDTH - 7, 8), WIDTH - 8})
    return (
        [(0, row, row) for row in rim]
        + [(1, row, WIDTH + row) for row in range(0, length, 8)]
        + [(2, row, WIDTH + length + row) for row in rim]
    )


def coefficient(plane, source, row, planes, coupling_ref, axial_ref, radial_ref, low_ref, high_ref):
    if source != 1:
        ref = low_ref if source == 0 else high_ref
        return ref[pl.ds((planes + plane) * WIDTH + row, 8), :]
    if plane < V * V:
        return coupling_ref[plane, pl.ds(row, 8), :]
    if plane == V * V + 2:
        return jnp.ones((8, 128), jnp.float32)
    return (axial_ref if plane == V * V else radial_ref)[pl.ds(row, 8), :]


def pack_radial_kernel(field_ref, coupling_ref, axial_ref, radial_ref, right_ref, left_ref):
    planes, length, _ = field_ref.shape
    groups = planes // (V * PER)
    lane = lanes_of((8, 128))

    def merge(tiles, offset):
        merged = pltpu.roll(tiles[0], offset, axis=1)
        for j in range(1, len(tiles)):
            merged = jnp.where(
                lane >= GROUP * j, pltpu.roll(tiles[j], (GROUP * j + offset) % 128, axis=1), merged
            )
        return merged

    def put(slot, row, tiles):
        right_ref[slot, pl.ds(row, 8), :] = merge(tiles, WIDTH)
        left_ref[slot, pl.ds(row, 8), :] = merge(tiles, 2)

    @pl.loop(0, groups)
    def _(group):
        for v in range(V):
            for row in range(0, length, 8):
                put(
                    group * V + v,
                    row,
                    [field_ref[(group * PER + j) * V + v, pl.ds(row, 8), :] for j in range(PER)],
                )

    for slot in range(-(-PLANES // PER)):
        for row in range(0, length, 8):
            tiles = [
                coefficient(plane, 1, row, planes, coupling_ref, axial_ref, radial_ref, None, None)
                for plane in range(slot * PER, min(PLANES, (slot + 1) * PER))
            ]
            put(groups * V + slot, row, tiles)


def pack_corner_kernel(left_ref, right_ref, up_ref, down_ref):
    slots, length, _ = left_ref.shape
    low = length - WIDTH
    for side, ref in ((0, left_ref), (1, right_ref)):
        for slot in range(slots):
            base = (side * slots + slot) * WIDTH
            for start in range(0, WIDTH, 8):
                size = min(8, WIDTH - start)
                up_ref[base + start : base + start + size, :] = ref[
                    slot, low + start : low + start + size, :
                ]
                down_ref[base + start : base + start + size, :] = ref[slot, start : start + size, :]


def weights_of(raw, viscosity):
    axial = raw[V * V] * (-TIME_STEP / 12.0)
    radial = raw[V * V + 1] * (-TIME_STEP / 12.0)
    inside = raw[V * V + 2]
    found = []
    for v in range(V):
        spread = inside * (viscosity[v] * (TIME_STEP / 12.0))
        for w in range(V):
            value = raw[v * V + w] * TIME_STEP
            found.append(value + (1.0 - 60.0 * spread) if v == w else value)
        for speed in (axial, radial):
            found.append(16.0 * spread + 8.0 * speed)
            found.append(16.0 * spread - 8.0 * speed)
            found.append(-spread - speed)
            found.append(speed - spread)
    return found


def steps_kernel(
    viscosity_ref,
    field_ref,
    coupling_ref,
    axial_ref,
    radial_ref,
    low_ref,
    high_ref,
    left_ref,
    right_ref,
    rim_low_ref,
    rim_high_ref,
    out_ref,
    now_ref,
    middle_ref,
    now_rim_ref,
    middle_rim_ref,
    weight_ref,
):
    planes, length, _ = field_ref.shape
    vectors = planes // V
    groups = vectors // PER
    slots = groups * V
    extended = length + 2 * WIDTH
    lane = lanes_of((8, 128))
    place = lane % GROUP
    viscosity = [viscosity_ref[v] for v in range(V)]

    @pl.loop(0, planes // 8)
    def _(block):
        for inner in range(8):
            plane = block * 8 + inner
            for source, row, target in chunks(length):
                if source == 1:
                    value = field_ref[plane, pl.ds(row, 8), :]
                else:
                    ref = low_ref if source == 0 else high_ref
                    value = ref[pl.ds(plane * WIDTH + row, 8), :]
                now_ref[plane, pl.ds(target, 8), :] = value

    packed = left_ref.shape[0]
    for side, own_ref in ((0, left_ref), (1, right_ref)):

        @pl.loop(0, packed)
        def _(slot):
            for source, row, target in chunks(length):
                if source == 1:
                    value = own_ref[slot, pl.ds(row, 8), :]
                else:
                    ref = rim_low_ref if source == 0 else rim_high_ref
                    value = ref[pl.ds((side * packed + slot) * WIDTH + row, 8), :]
                now_rim_ref[side, slot, pl.ds(target, 8), :] = value

    for source, row, target in chunks(length):
        raw = [
            coefficient(
                plane, source, row, planes, coupling_ref, axial_ref, radial_ref, low_ref, high_ref
            )
            for plane in range(PLANES)
        ]
        for index, value in enumerate(weights_of(raw, viscosity)):
            weight_ref[0, index, pl.ds(target, 8), :] = value

    @pl.loop(0, extended // 8)
    def _(block):
        start = pl.multiple_of(block * 8, 8)
        for side in range(2):
            raw = []
            for plane in range(PLANES):
                tile = now_rim_ref[side, slots + plane // PER, pl.ds(start, 8), :]
                tile = pltpu.roll(tile, (128 - GROUP * (plane % PER)) % 128, axis=1)
                tile = jnp.where(lane < GROUP, tile, 0.0)
                reach = GROUP
                while reach < 128:
                    tile = tile + pltpu.roll(tile, reach, axis=1)
                    reach *= 2
                raw.append(tile)
            for index, value in enumerate(weights_of(raw, viscosity)):
                weight_ref[1 + side, index, pl.ds(start, 8), :] = value

    def euler(v, kind, start, count, centers, vertical, sideways):
        def weight(index):
            return weight_ref[kind, v * (V + 8) + index, pl.ds(start, 8), :]

        totals = None
        for w in range(V):
            factor = weight(w)
            terms = [factor * centers[i][w] for i in range(count)]
            totals = terms if totals is None else [a + b for a, b in zip(totals, terms)]
        for index, step in enumerate((1, -1, 2, -2)):
            factor = weight(V + index)
            totals = [totals[i] + factor * vertical(i, step) for i in range(count)]
        for index, step in enumerate((1, -1, 2, -2)):
            factor = weight(V + 4 + index)
            totals = [totals[i] + factor * sideways(i, step) for i in range(count)]
        return totals

    for section in range(1, SECTIONS + 1):
        odd = section % 2 == 1
        last = section == SECTIONS
        source, source_rim = (now_ref, now_rim_ref) if odd else (middle_ref, middle_rim_ref)
        target, target_rim = (middle_ref, middle_rim_ref) if odd else (now_ref, now_rim_ref)
        first = 2 * section
        blocks = -(-(extended - 2 * first) // 8)

        @pl.loop(0, groups * blocks)
        def _(index):
            group, block = index // blocks, index % blocks
            start = first + block * 8
            joints = []
            for v in range(V):
                slot = group * V + v
                own = None
                for j in range(PER):
                    tile = source[(group * PER + j) * V + v, pl.ds(start, 8), :]
                    tile = pltpu.roll(tile, (GROUP * j + WIDTH) % 128, axis=1)
                    own = tile if own is None else jnp.where(lane >= GROUP * j, tile, own)
                left = source_rim[0, slot, pl.ds(start, 8), :]
                right = source_rim[1, slot, pl.ds(start, 8), :]
                inner = (place == WIDTH) | (place == WIDTH + 1)
                joints.append(jnp.where(inner, pltpu.roll(right, WIDTH - 2, axis=1), left))
                if not last:
                    source_rim[0, slot, pl.ds(start, 8), :] = jnp.where(inner, own, left)
                    source_rim[1, slot, pl.ds(start, 8), :] = jnp.where(
                        place < 2, pltpu.roll(own, 128 - (WIDTH - 2), axis=1), right
                    )

            if not last:
                for side in range(2):
                    slot = group * V
                    centers = [
                        [source_rim[side, slot + w, pl.ds(start, 8), :] for w in range(V)]
                    ]
                    for v in range(V):
                        (value,) = euler(
                            v,
                            1 + side,
                            start,
                            1,
                            centers,
                            lambda i, step: source_rim[side, slot + v, pl.ds(start + step, 8), :],
                            lambda i, step: pltpu.roll(centers[0][v], (128 - step) % 128, axis=1),
                        )
                        if not odd:
                            value = 0.5 * (value + target_rim[side, slot + v, pl.ds(start, 8), :])
                        target_rim[side, slot + v, pl.ds(start, 8), :] = value

            @pl.loop(0, PER // TOGETHER)
            def _(part):
                bases = [(group * PER + part * TOGETHER + i) * V for i in range(TOGETHER)]
                centers = [
                    [source[base + w, pl.ds(start, 8), :] for w in range(V)] for base in bases
                ]
                for v in range(V):
                    rims = [
                        pltpu.roll(
                            joints[v],
                            256 - WIDTH - GROUP * (part * TOGETHER + i),
                            axis=1,
                        )
                        for i in range(TOGETHER)
                    ]
                    edges = {1: lane == 0, 2: lane <= 1, -1: lane == 127, -2: lane >= 126}

                    def sideways(i, step):
                        tile = jnp.where(edges[step], rims[i], centers[i][v])
                        return pltpu.roll(tile, (128 - step) % 128, axis=1)

                    values = euler(
                        v,
                        0,
                        start,
                        TOGETHER,
                        centers,
                        lambda i, step: source[bases[i] + v, pl.ds(start + step, 8), :],
                        sideways,
                    )
                    for i in range(TOGETHER):
                        value = values[i]
                        if not odd:
                            value = 0.5 * (value + target[bases[i] + v, pl.ds(start, 8), :])
                        if last:
                            out_ref[bases[i] + v, pl.ds(start - WIDTH, 8), :] = value
                        else:
                            target[bases[i] + v, pl.ds(start, 8), :] = value


TOGETHER = 8


def factor_kernel(parts_ref, factor_ref, inverse_ref, *, rows_all):
    total = jnp.sum(parts_ref[...], axis=0) * (1.0 / rows_all)
    order = factor_ref.shape[0]
    lane = lax.broadcasted_iota(jnp.int32, (order, 128), 1)
    row = lax.broadcasted_iota(jnp.int32, (order, 128), 0)
    pieces = [total] + [pltpu.roll(total, 128 - 32 * i, axis=1) for i in range(1, 4)]
    work = jnp.concatenate(pieces, axis=0)
    work = jnp.where(lane < order, work, jnp.where(lane == row + order, 1.0, 0.0))
    for j in range(order - 1):
        pivot_row = work[j : j + 1, :]
        scale = pivot_row / pivot_row[:, j : j + 1]
        column = jnp.where(row > j, jnp.broadcast_to(work[:, j : j + 1], work.shape), 0.0)
        work = work - column * scale
    diagonal = jnp.sum(jnp.where(lane == row, work, 0.0), axis=1, keepdims=True)
    work = work / jnp.sqrt(diagonal)
    factor_ref[...] = jnp.where(lane >= row, work, 0.0)[:, :order]
    inverse_ref[...] = jnp.where(lane <= row, pltpu.roll(work, 128 - order, axis=1), 0.0)[:, :order]


def factor_and_inverse(parts, order, rows_all):
    square = jax.ShapeDtypeStruct((order, order), jnp.float32)
    return pl.pallas_call(
        functools.partial(factor_kernel, rows_all=rows_all),
        out_shape=(square, square),
        name="factor",
    )(parts)


def shape_of(*dims):
    return jax.ShapeDtypeStruct(dims, jnp.float32)


def shifted(block, axis, step):
    size = lax.axis_size(axis)
    return lax.ppermute(
        block, axis, [(i, i + step) for i in range(size) if 0 <= i + step < size]
    )


def steps_call(viscosity, local, *received):
    planes, length, columns = local[0].shape
    rows = length + 2 * WIDTH + 8
    return pl.pallas_call(
        steps_kernel,
        in_specs=[pl.BlockSpec(memory_space=pltpu.SMEM)] + whole(10),
        out_specs=whole(1)[0],
        out_shape=shape_of(planes, length, columns),
        scratch_shapes=[
            pltpu.VMEM((planes, rows, columns), jnp.float32),
            pltpu.VMEM((planes, rows, columns), jnp.float32),
            pltpu.VMEM((2, received[2].shape[0], rows, columns), jnp.float32),
            pltpu.VMEM((2, planes // PER, rows, columns), jnp.float32),
            pltpu.VMEM((3, WEIGHTS, rows, columns), jnp.float32),
        ],
        compiler_params=pltpu.CompilerParams(vmem_limit_bytes=VMEM_LIMIT),
        name="steps",
    )(viscosity, *local, *received)


def per_device(forcing, vel_axial, vel_radial, coupling, viscosity):
    vectors, variables, length, columns = forcing.shape
    planes = vectors * variables
    field = forcing.reshape(planes, length, columns)
    local = (field, coupling.reshape(V * V, length, columns), vel_axial, vel_radial)
    params = pltpu.CompilerParams(vmem_limit_bytes=VMEM_LIMIT)

    strip = shape_of((planes + PLANES) * WIDTH, columns)
    up, down = pl.pallas_call(
        pack_axial_kernel,
        in_specs=whole(4),
        out_specs=whole(2),
        out_shape=(strip, strip),
        compiler_params=params,
        name="pack_axial",
    )(*local)
    low = shifted(up, "ax", 1)
    high = shifted(down, "ax", -1)

    rim = shape_of(planes // PER + -(-PLANES // PER), length, columns)
    to_right, to_left = pl.pallas_call(
        pack_radial_kernel,
        in_specs=whole(4),
        out_specs=whole(2),
        out_shape=(rim, rim),
        compiler_params=params,
        name="pack_radial",
    )(*local)
    left = shifted(to_right, "rad", 1)
    right = shifted(to_left, "rad", -1)

    corner = shape_of(2 * rim.shape[0] * WIDTH, columns)
    rim_up, rim_down = pl.pallas_call(
        pack_corner_kernel,
        in_specs=whole(2),
        out_specs=whole(2),
        out_shape=(corner, corner),
        compiler_params=params,
        name="pack_corner",
    )(left, right)
    rim_low = shifted(rim_up, "ax", 1)
    rim_high = shifted(rim_down, "ax", -1)
    response = steps_call(viscosity, local, low, high, left, right, rim_low, rim_high)

    flattened = response.reshape(vectors, variables * length * columns)
    devices = lax.axis_size("ax") * lax.axis_size("rad")
    rows_all = variables * length * columns * devices
    local_gram = jnp.dot(flattened, flattened.T, precision=lax.Precision.HIGHEST)
    packed = jnp.concatenate([local_gram[8 * i : 8 * i + 8] for i in range(4)], axis=1)
    copies = jnp.broadcast_to(packed, (devices, 8, 128))
    parts = lax.all_to_all(copies, ("ax", "rad"), 0, 0)
    upper_factor, lower_inverse = factor_and_inverse(parts, vectors, rows_all)
    basis = jnp.dot(lower_inverse, flattened, precision=lax.Precision.HIGHEST).reshape(forcing.shape)
    return (basis, upper_factor)


def solution(mesh):
    return jax.shard_map(
        per_device,
        mesh=mesh,
        in_specs=(
            P(None, None, "ax", "rad"),
            P("ax", "rad"),
            P("ax", "rad"),
            P(None, None, "ax", "rad"),
            P(),
        ),
        out_specs=(P(None, None, "ax", "rad"), P()),
        check_vma=False,
    )
```

```python
import functools

import jax
import jax.numpy as jnp
from jax import lax
from jax.experimental import pallas as pl
from jax.experimental.pallas import tpu as pltpu
from jax.sharding import PartitionSpec as P

STEPS = 3
TIME_STEP = 0.8
SECTIONS = 2 * STEPS
WIDTH = 2 * SECTIONS
V = 5
GROUP = 16
PER = 128 // GROUP
PLANES = V * V + 3
WEIGHTS = V * (V + 8)
VMEM_LIMIT = 56 << 20


def whole(count):
    return [pl.BlockSpec(memory_space=pltpu.VMEM) for _ in range(count)]


def lanes_of(shape):
    return lax.broadcasted_iota(jnp.int32, shape, 1)


def pack_axial_kernel(field_ref, coupling_ref, axial_ref, radial_ref, up_ref, down_ref):
    planes, length, _ = field_ref.shape
    low = length - WIDTH

    def put(slot, read):
        base = slot * WIDTH
        for start in range(0, WIDTH, 8):
            size = min(8, WIDTH - start)
            up_ref[pl.ds(base + start, size), :] = read(low + start, size)
            down_ref[pl.ds(base + start, size), :] = read(start, size)

    @pl.loop(0, planes // 8)
    def _(block):
        for inner in range(8):
            plane = block * 8 + inner
            put(plane, lambda start, size: field_ref[plane, pl.ds(start, size), :])

    for plane in range(V * V):
        put(planes + plane, lambda start, size: coupling_ref[plane, pl.ds(start, size), :])
    put(planes + V * V, lambda start, size: axial_ref[pl.ds(start, size), :])
    put(planes + V * V + 1, lambda start, size: radial_ref[pl.ds(start, size), :])
    put(planes + V * V + 2, lambda start, size: jnp.ones((size, 128), jnp.float32))


def chunks(length):
    rim = sorted({*range(0, WIDTH - 7, 8), WIDTH - 8})
    return (
        [(0, row, row) for row in rim]
        + [(1, row, WIDTH + row) for row in range(0, length, 8)]
        + [(2, row, WIDTH + length + row) for row in rim]
    )


def coefficient(plane, source, row, planes, coupling_ref, axial_ref, radial_ref, low_ref, high_ref):
    if source != 1:
        ref = low_ref if source == 0 else high_ref
        return ref[pl.ds((planes + plane) * WIDTH + row, 8), :]
    if plane < V * V:
        return coupling_ref[plane, pl.ds(row, 8), :]
    if plane == V * V + 2:
        return jnp.ones((8, 128), jnp.float32)
    return (axial_ref if plane == V * V else radial_ref)[pl.ds(row, 8), :]


def pack_radial_kernel(field_ref, coupling_ref, axial_ref, radial_ref, right_ref, left_ref):
    planes, length, _ = field_ref.shape
    groups = planes // (V * PER)
    lane = lanes_of((8, 128))

    def merge(tiles, offset):
        merged = pltpu.roll(tiles[0], offset, axis=1)
        for j in range(1, len(tiles)):
            merged = jnp.where(
                lane >= GROUP * j, pltpu.roll(tiles[j], (GROUP * j + offset) % 128, axis=1), merged
            )
        return merged

    def put(slot, row, tiles):
        right_ref[slot, pl.ds(row, 8), :] = merge(tiles, WIDTH)
        left_ref[slot, pl.ds(row, 8), :] = merge(tiles, 2)

    @pl.loop(0, groups)
    def _(group):
        for v in range(V):
            for row in range(0, length, 8):
                put(
                    group * V + v,
                    row,
                    [field_ref[(group * PER + j) * V + v, pl.ds(row, 8), :] for j in range(PER)],
                )

    for slot in range(-(-PLANES // PER)):
        for row in range(0, length, 8):
            tiles = [
                coefficient(plane, 1, row, planes, coupling_ref, axial_ref, radial_ref, None, None)
                for plane in range(slot * PER, min(PLANES, (slot + 1) * PER))
            ]
            put(groups * V + slot, row, tiles)


def pack_corner_kernel(left_ref, right_ref, up_ref, down_ref):
    slots, length, _ = left_ref.shape
    low = length - WIDTH
    for side, ref in ((0, left_ref), (1, right_ref)):
        for slot in range(slots):
            base = (side * slots + slot) * WIDTH
            for start in range(0, WIDTH, 8):
                size = min(8, WIDTH - start)
                up_ref[base + start : base + start + size, :] = ref[
                    slot, low + start : low + start + size, :
                ]
                down_ref[base + start : base + start + size, :] = ref[slot, start : start + size, :]


def neighbours(spread, speed):
    return (
        16.0 * spread + 8.0 * speed,
        16.0 * spread - 8.0 * speed,
        -spread - speed,
        speed - spread,
    )


def weights_of(raw, viscosity):
    axial = raw[V * V] * (-TIME_STEP / 12.0)
    radial = raw[V * V + 1] * (-TIME_STEP / 12.0)
    inside = raw[V * V + 2]
    found = []
    for v in range(V):
        spread = inside * (viscosity[v] * (TIME_STEP / 12.0))
        for w in range(V):
            value = raw[v * V + w] * TIME_STEP
            found.append(value + (1.0 - 60.0 * spread) if v == w else value)
        for speed in (axial, radial):
            found.extend(neighbours(spread, speed))
    return found


def steps_kernel(
    viscosity_ref,
    field_ref,
    coupling_ref,
    axial_ref,
    radial_ref,
    low_ref,
    high_ref,
    left_ref,
    right_ref,
    rim_low_ref,
    rim_high_ref,
    out_ref,
    now_ref,
    middle_ref,
    now_rim_ref,
    middle_rim_ref,
    weight_ref,
    edge_ref,
    first_ref,
    second_ref,
    band_ref,
):
    planes, length, _ = field_ref.shape
    vectors = planes // V
    groups = vectors // PER
    slots = groups * V
    extended = length + 2 * WIDTH
    lane = lanes_of((8, 128))
    place = lane % GROUP
    viscosity = [viscosity_ref[v] for v in range(V)]

    def spread_out(tile):
        reach = GROUP
        while reach < 128:
            tile = tile + pltpu.roll(tile, reach, axis=1)
            reach *= 2
        return tile

    shape = (128, 256)
    offset = lax.broadcasted_iota(jnp.int32, shape, 0) - lax.broadcasted_iota(
        jnp.int32, shape, 1
    )
    offset_column = lax.broadcasted_iota(jnp.int32, shape, 1)
    band = jnp.zeros(shape, jnp.float32)
    for gap, odd_part, even_part in ((1, 8.0, 16.0), (-1, -8.0, 16.0), (2, -1.0, -1.0), (-2, 1.0, -1.0)):
        band = jnp.where((offset == gap) & (offset_column < 128), odd_part, band)
        band = jnp.where((offset + 128 == gap) & (offset_column >= 128), even_part, band)
    for part in range(SPLIT):
        band_ref[pl.ds(128 * part, 128), :] = band.astype(jnp.bfloat16)

    @pl.loop(0, planes // 8)
    def _(block):
        for inner in range(8):
            plane = block * 8 + inner
            for source, row, target in chunks(length):
                if source == 1:
                    value = field_ref[plane, pl.ds(row, 8), :]
                else:
                    ref = low_ref if source == 0 else high_ref
                    value = ref[pl.ds(plane * WIDTH + row, 8), :]
                now_ref[plane, pl.ds(target, 8), :] = value

    packed = left_ref.shape[0]
    for side, own_ref in ((0, left_ref), (1, right_ref)):

        @pl.loop(0, packed)
        def _(slot):
            for source, row, target in chunks(length):
                if source == 1:
                    value = own_ref[slot, pl.ds(row, 8), :]
                else:
                    ref = rim_low_ref if source == 0 else rim_high_ref
                    value = ref[pl.ds((side * packed + slot) * WIDTH + row, 8), :]
                now_rim_ref[side, slot, pl.ds(target, 8), :] = value

    for source, row, target in chunks(length):
        raw = [
            coefficient(
                plane, source, row, planes, coupling_ref, axial_ref, radial_ref, low_ref, high_ref
            )
            for plane in range(PLANES)
        ]
        for index, value in enumerate(weights_of(raw, viscosity)):
            if index % (V + 8) < V + 4:
                weight_ref[0, index, pl.ds(target, 8), :] = value
        near = (lane >= WIDTH - 2) & (lane < WIDTH + 2)
        edge_speed, edge_inside = [
            spread_out(jnp.where(near, pltpu.roll(raw[plane], WIDTH, axis=1), 0.0))
            for plane in (V * V + 1, V * V + 2)
        ]
        edge_speed = edge_speed * (-TIME_STEP / 12.0)
        keeps = (
            place == WIDTH - 1,
            place == WIDTH,
            (place == WIDTH - 2) | (place == WIDTH - 1),
            (place == WIDTH) | (place == WIDTH + 1),
        )
        for v in range(V):
            spread = edge_inside * (viscosity[v] * (TIME_STEP / 12.0))
            for kind, value in enumerate(neighbours(spread, edge_speed)):
                edge_ref[v * 4 + kind, pl.ds(target, 8), :] = jnp.where(keeps[kind], value, 0.0)
        radial = raw[V * V + 1] * (-TIME_STEP / 12.0)
        weight_ref[0, V + 4, pl.ds(target, 8), :] = radial
        for v in range(V):
            weight_ref[0, v * (V + 8) + V + 5, pl.ds(target, 8), :] = raw[V * V + 2] * (
                viscosity[v] * (TIME_STEP / 12.0)
            )

    @pl.loop(0, extended // 8)
    def _(block):
        start = pl.multiple_of(block * 8, 8)
        for side in range(2):
            raw = []
            for plane in range(PLANES):
                tile = now_rim_ref[side, slots + plane // PER, pl.ds(start, 8), :]
                tile = pltpu.roll(tile, (128 - GROUP * (plane % PER)) % 128, axis=1)
                raw.append(spread_out(jnp.where(lane < GROUP, tile, 0.0)))
            for index, value in enumerate(weights_of(raw, viscosity)):
                weight_ref[1 + side, index, pl.ds(start, 8), :] = value

    def euler(v, kind, start, count, centers, vertical, sideways):
        def weight(index):
            return weight_ref[kind, v * (V + 8) + index, pl.ds(start, 8), :]

        totals = None
        for w in range(V):
            factor = weight(w)
            terms = [factor * centers[i][w] for i in range(count)]
            totals = terms if totals is None else [a + b for a, b in zip(totals, terms)]
        for index, step in enumerate((1, -1, 2, -2)):
            factor = weight(V + index)
            totals = [totals[i] + factor * vertical(i, step) for i in range(count)]
        if kind > 0:
            for index, step in enumerate((1, -1, 2, -2)):
                factor = weight(V + 4 + index)
                totals = [totals[i] + factor * sideways(i, step) for i in range(count)]
            return totals
        speed, spread = weight_ref[0, V + 4, pl.ds(start, 8), :], weight(V + 5)
        for i in range(count):
            one, two, rim = sideways(i, 0)
            totals[i] = ((totals[i] + rim) + speed * one) + spread * two
        return totals

    for section in range(1, SECTIONS + 1):
        odd = section % 2 == 1
        last = section == SECTIONS
        source, source_rim = (now_ref, now_rim_ref) if odd else (middle_ref, middle_rim_ref)
        target, target_rim = (middle_ref, middle_rim_ref) if odd else (now_ref, now_rim_ref)
        first = 2 * section
        blocks = -(-(extended - 2 * first) // 8)
        low_row, high_row = first // 8 * 8, -(-(extended - first) // 8) * 8

        @pl.loop(0, planes // BATCH)
        def _(batch):
            here = pl.ds(batch * BATCH, BATCH)
            rest = source[here, low_row:high_row, :].reshape(BATCH * (high_row - low_row), 128)
            halves = []
            for part in range(SPLIT):
                halves.append(rest.astype(jnp.bfloat16))
                if part < SPLIT - 1:
                    rest = rest - halves[-1].astype(jnp.float32)
            both = jnp.dot(
                jnp.concatenate(halves, axis=1), band_ref[...], preferred_element_type=jnp.float32
            )
            first_ref[here, low_row:high_row, :] = both[:, :128].reshape(BATCH, -1, 128)
            second_ref[here, low_row:high_row, :] = both[:, 128:].reshape(BATCH, -1, 128)

        @pl.loop(0, groups * blocks)
        def _(index):
            group, block = index // blocks, index % blocks
            start = first + block * 8
            joints = []
            for v in range(V):
                slot = group * V + v
                own = None
                for j in range(PER):
                    tile = source[(group * PER + j) * V + v, pl.ds(start, 8), :]
                    tile = pltpu.roll(tile, (GROUP * j + WIDTH) % 128, axis=1)
                    own = tile if own is None else jnp.where(lane >= GROUP * j, tile, own)
                left = source_rim[0, slot, pl.ds(start, 8), :]
                right = source_rim[1, slot, pl.ds(start, 8), :]
                inner = (place == WIDTH) | (place == WIDTH + 1)
                joint = jnp.where(inner, pltpu.roll(right, WIDTH - 2, axis=1), left)
                joints.append(
                    sum(
                        edge_ref[v * 4 + index, pl.ds(start, 8), :]
                        * pltpu.roll(joint, (128 - step) % 128, axis=1)
                        for index, step in enumerate((1, -1, 2, -2))
                    )
                )
                if not last:
                    source_rim[0, slot, pl.ds(start, 8), :] = jnp.where(inner, own, left)
                    source_rim[1, slot, pl.ds(start, 8), :] = jnp.where(
                        place < 2, pltpu.roll(own, 128 - (WIDTH - 2), axis=1), right
                    )

            if not last:
                for side in range(2):
                    slot = group * V
                    centers = [
                        [source_rim[side, slot + w, pl.ds(start, 8), :] for w in range(V)]
                    ]
                    for v in range(V):
                        (value,) = euler(
                            v,
                            1 + side,
                            start,
                            1,
                            centers,
                            lambda i, step: source_rim[side, slot + v, pl.ds(start + step, 8), :],
                            lambda i, step: pltpu.roll(centers[0][v], (128 - step) % 128, axis=1),
                        )
                        if not odd:
                            value = 0.5 * (value + target_rim[side, slot + v, pl.ds(start, 8), :])
                        target_rim[side, slot + v, pl.ds(start, 8), :] = value

            for part in range(PER // TOGETHER):
                bases = [(group * PER + part * TOGETHER + i) * V for i in range(TOGETHER)]
                centers = [
                    [source[base + w, pl.ds(start, 8), :] for w in range(V)] for base in bases
                ]
                for v in range(V):
                    rims = [
                        pltpu.roll(
                            joints[v],
                            (256 - WIDTH - GROUP * (part * TOGETHER + i)) % 128,
                            axis=1,
                        )
                        for i in range(TOGETHER)
                    ]
                    edge = (lane < 2) | (lane >= 126)

                    def sideways(i, step):
                        plane = bases[i] + v
                        return (
                            first_ref[plane, pl.ds(start, 8), :],
                            second_ref[plane, pl.ds(start, 8), :],
                            jnp.where(edge, rims[i], 0.0),
                        )

                    values = euler(
                        v,
                        0,
                        start,
                        TOGETHER,
                        centers,
                        lambda i, step: source[bases[i] + v, pl.ds(start + step, 8), :],
                        sideways,
                    )
                    for i in range(TOGETHER):
                        value = values[i]
                        if not odd:
                            value = 0.5 * (value + target[bases[i] + v, pl.ds(start, 8), :])
                        if last:
                            out_ref[bases[i] + v, pl.ds(start - WIDTH, 8), :] = value
                        else:
                            target[bases[i] + v, pl.ds(start, 8), :] = value


TOGETHER = 8
SPLIT = 2
BATCH = 80


def factor_kernel(parts_ref, factor_ref, inverse_ref, *, rows_all):
    total = jnp.sum(parts_ref[...], axis=0) * (1.0 / rows_all)
    order = factor_ref.shape[0]
    lane = lax.broadcasted_iota(jnp.int32, (order, 128), 1)
    row = lax.broadcasted_iota(jnp.int32, (order, 128), 0)
    pieces = [total] + [pltpu.roll(total, 128 - 32 * i, axis=1) for i in range(1, 4)]
    work = jnp.concatenate(pieces, axis=0)
    work = jnp.where(lane < order, work, jnp.where(lane == row + order, 1.0, 0.0))
    for j in range(order - 1):
        pivot_row = work[j : j + 1, :]
        scale = pivot_row / pivot_row[:, j : j + 1]
        column = jnp.where(row > j, jnp.broadcast_to(work[:, j : j + 1], work.shape), 0.0)
        work = work - column * scale
    diagonal = jnp.sum(jnp.where(lane == row, work, 0.0), axis=1, keepdims=True)
    work = work / jnp.sqrt(diagonal)
    factor_ref[...] = jnp.where(lane >= row, work, 0.0)[:, :order]
    inverse_ref[...] = jnp.where(lane <= row, pltpu.roll(work, 128 - order, axis=1), 0.0)[:, :order]


def factor_and_inverse(parts, order, rows_all):
    square = jax.ShapeDtypeStruct((order, order), jnp.float32)
    return pl.pallas_call(
        functools.partial(factor_kernel, rows_all=rows_all),
        out_shape=(square, square),
        name="factor",
    )(parts)


def shape_of(*dims):
    return jax.ShapeDtypeStruct(dims, jnp.float32)


def shifted(block, axis, step):
    size = lax.axis_size(axis)
    return lax.ppermute(
        block, axis, [(i, i + step) for i in range(size) if 0 <= i + step < size]
    )


def steps_call(viscosity, local, *received):
    planes, length, columns = local[0].shape
    rows = length + 2 * WIDTH + 8
    return pl.pallas_call(
        steps_kernel,
        in_specs=[pl.BlockSpec(memory_space=pltpu.SMEM)] + whole(10),
        out_specs=whole(1)[0],
        out_shape=shape_of(planes, length, columns),
        scratch_shapes=[
            pltpu.VMEM((planes, rows, columns), jnp.float32),
            pltpu.VMEM((planes, rows, columns), jnp.float32),
            pltpu.VMEM((2, received[2].shape[0], rows, columns), jnp.float32),
            pltpu.VMEM((2, planes // PER, rows, columns), jnp.float32),
            pltpu.VMEM((3, WEIGHTS, rows, columns), jnp.float32),
            pltpu.VMEM((4 * V, rows, columns), jnp.float32),
            pltpu.VMEM((planes, rows, columns), jnp.float32),
            pltpu.VMEM((planes, rows, columns), jnp.float32),
            pltpu.VMEM((SPLIT * columns, 2 * columns), jnp.bfloat16),
        ],
        compiler_params=pltpu.CompilerParams(vmem_limit_bytes=VMEM_LIMIT),
        name="steps",
    )(viscosity, *local, *received)


def per_device(forcing, vel_axial, vel_radial, coupling, viscosity):
    vectors, variables, length, columns = forcing.shape
    planes = vectors * variables
    field = forcing.reshape(planes, length, columns)
    local = (field, coupling.reshape(V * V, length, columns), vel_axial, vel_radial)
    params = pltpu.CompilerParams(vmem_limit_bytes=VMEM_LIMIT)

    strip = shape_of((planes + PLANES) * WIDTH, columns)
    up, down = pl.pallas_call(
        pack_axial_kernel,
        in_specs=whole(4),
        out_specs=whole(2),
        out_shape=(strip, strip),
        compiler_params=params,
        name="pack_axial",
    )(*local)
    low = shifted(up, "ax", 1)
    high = shifted(down, "ax", -1)

    rim = shape_of(planes // PER + -(-PLANES // PER), length, columns)
    to_right, to_left = pl.pallas_call(
        pack_radial_kernel,
        in_specs=whole(4),
        out_specs=whole(2),
        out_shape=(rim, rim),
        compiler_params=params,
        name="pack_radial",
    )(*local)
    left = shifted(to_right, "rad", 1)
    right = shifted(to_left, "rad", -1)

    corner = shape_of(2 * rim.shape[0] * WIDTH, columns)
    rim_up, rim_down = pl.pallas_call(
        pack_corner_kernel,
        in_specs=whole(2),
        out_specs=whole(2),
        out_shape=(corner, corner),
        compiler_params=params,
        name="pack_corner",
    )(left, right)
    rim_low = shifted(rim_up, "ax", 1)
    rim_high = shifted(rim_down, "ax", -1)
    response = steps_call(viscosity, local, low, high, left, right, rim_low, rim_high)

    flattened = response.reshape(vectors, variables * length * columns)
    devices = lax.axis_size("ax") * lax.axis_size("rad")
    rows_all = variables * length * columns * devices
    local_gram = jnp.dot(flattened, flattened.T, precision=lax.Precision.HIGHEST)
    packed = jnp.concatenate([local_gram[8 * i : 8 * i + 8] for i in range(4)], axis=1)
    copies = jnp.broadcast_to(packed, (devices, 8, 128))
    parts = lax.all_to_all(copies, ("ax", "rad"), 0, 0)
    upper_factor, lower_inverse = factor_and_inverse(parts, vectors, rows_all)
    basis = jnp.dot(lower_inverse, flattened, precision=lax.Precision.HIGHEST).reshape(forcing.shape)
    return (basis, upper_factor)


def solution(mesh):
    return jax.shard_map(
        per_device,
        mesh=mesh,
        in_specs=(
            P(None, None, "ax", "rad"),
            P("ax", "rad"),
            P("ax", "rad"),
            P(None, None, "ax", "rad"),
            P(),
        ),
        out_specs=(P(None, None, "ax", "rad"), P()),
        check_vma=False,
    )
```

```python
import functools

import jax
import jax.numpy as jnp
from jax import lax
from jax.experimental import pallas as pl
from jax.experimental.pallas import tpu as pltpu
from jax.sharding import PartitionSpec as P

STEPS = 3
TIME_STEP = 0.8
SECTIONS = 2 * STEPS
WIDTH = 2 * SECTIONS
V = 5
GROUP = 16
PARTS = 2
PER = 128 // GROUP
PLANES = V * V + 3
WEIGHTS = V * (V + 8)
VMEM_LIMIT = 56 << 20


def whole(count):
    return [pl.BlockSpec(memory_space=pltpu.VMEM) for _ in range(count)]


def lanes_of(shape):
    return lax.broadcasted_iota(jnp.int32, shape, 1)


def pack_axial_kernel(field_ref, coupling_ref, axial_ref, radial_ref, *refs, begin, end):
    up_ref, down_ref = refs[-2:]
    length = field_ref.shape[1]
    low = length - WIDTH

    def put(slot, read):
        base = slot * WIDTH
        for start in range(0, WIDTH, 8):
            size = min(8, WIDTH - start)
            up_ref[pl.ds(base + start, size), :] = read(low + start, size)
            down_ref[pl.ds(base + start, size), :] = read(start, size)

    @pl.loop(0, (end - begin) // 8)
    def _(block):
        for inner in range(8):
            slot = block * 8 + inner
            put(slot, lambda start, size: field_ref[begin + slot, pl.ds(start, size), :])

    if begin > 0:
        return
    for plane in range(V * V):
        put(end + plane, lambda start, size: coupling_ref[plane, pl.ds(start, size), :])
    put(end + V * V, lambda start, size: axial_ref[pl.ds(start, size), :])
    put(end + V * V + 1, lambda start, size: radial_ref[pl.ds(start, size), :])
    put(end + V * V + 2, lambda start, size: jnp.ones((size, 128), jnp.float32))


def chunks(length):
    rim = sorted({*range(0, WIDTH - 7, 8), WIDTH - 8})
    return (
        [(0, row, row) for row in rim]
        + [(1, row, WIDTH + row) for row in range(0, length, 8)]
        + [(2, row, WIDTH + length + row) for row in rim]
    )


def coefficient(plane, source, row, planes, coupling_ref, axial_ref, radial_ref, low_ref, high_ref):
    if source != 1:
        ref = low_ref if source == 0 else high_ref
        return ref[pl.ds((planes + plane) * WIDTH + row, 8), :]
    if plane < V * V:
        return coupling_ref[plane, pl.ds(row, 8), :]
    if plane == V * V + 2:
        return jnp.ones((8, 128), jnp.float32)
    return (axial_ref if plane == V * V else radial_ref)[pl.ds(row, 8), :]


def pack_radial_kernel(field_ref, coupling_ref, axial_ref, radial_ref, right_ref, left_ref):
    planes, length, _ = field_ref.shape
    groups = planes // (V * PER)
    lane = lanes_of((8, 128))

    def merge(tiles, offset):
        merged = pltpu.roll(tiles[0], offset, axis=1)
        for j in range(1, len(tiles)):
            merged = jnp.where(
                lane >= GROUP * j, pltpu.roll(tiles[j], (GROUP * j + offset) % 128, axis=1), merged
            )
        return merged

    def put(slot, row, tiles):
        right_ref[slot, pl.ds(row, 8), :] = merge(tiles, WIDTH)
        left_ref[slot, pl.ds(row, 8), :] = merge(tiles, 2)

    @pl.loop(0, groups)
    def _(group):
        for v in range(V):
            for row in range(0, length, 8):
                put(
                    group * V + v,
                    row,
                    [field_ref[(group * PER + j) * V + v, pl.ds(row, 8), :] for j in range(PER)],
                )

    for slot in range(-(-PLANES // PER)):
        for row in range(0, length, 8):
            tiles = [
                coefficient(plane, 1, row, planes, coupling_ref, axial_ref, radial_ref, None, None)
                for plane in range(slot * PER, min(PLANES, (slot + 1) * PER))
            ]
            put(groups * V + slot, row, tiles)


def pack_corner_kernel(left_ref, right_ref, up_ref, down_ref, done_ref):
    done_ref[...] = jnp.zeros(done_ref.shape, jnp.float32)
    slots, length, _ = left_ref.shape
    low = length - WIDTH
    for side, ref in ((0, left_ref), (1, right_ref)):
        for slot in range(slots):
            base = (side * slots + slot) * WIDTH
            for start in range(0, WIDTH, 8):
                size = min(8, WIDTH - start)
                up_ref[base + start : base + start + size, :] = ref[
                    slot, low + start : low + start + size, :
                ]
                down_ref[base + start : base + start + size, :] = ref[slot, start : start + size, :]


def neighbours(spread, speed):
    return (
        16.0 * spread + 8.0 * speed,
        16.0 * spread - 8.0 * speed,
        -spread - speed,
        speed - spread,
    )


def weights_of(raw, viscosity):
    axial = raw[V * V] * (-TIME_STEP / 12.0)
    radial = raw[V * V + 1] * (-TIME_STEP / 12.0)
    inside = raw[V * V + 2]
    found = []
    for v in range(V):
        spread = inside * (viscosity[v] * (TIME_STEP / 12.0))
        for w in range(V):
            value = raw[v * V + w] * TIME_STEP
            found.append(value + (1.0 - 60.0 * spread) if v == w else value)
        for speed in (axial, radial):
            found.extend(neighbours(spread, speed))
    return found


def steps_kernel(
    viscosity_ref,
    field_ref,
    coupling_ref,
    axial_ref,
    radial_ref,
    low_ref,
    high_ref,
    first_low_ref,
    first_high_ref,
    left_ref,
    right_ref,
    rim_low_ref,
    rim_high_ref,
    *rest,
    turn,
):
    (
        out_ref,
        now_ref,
        middle_ref,
        now_rim_ref,
        middle_rim_ref,
        weight_ref,
        edge_ref,
        first_ref,
        second_ref,
        band_ref,
    ) = rest[-10:]
    planes, length = field_ref.shape[0] // PARTS, field_ref.shape[1]
    vectors = planes // V
    groups = vectors // PER
    slots = groups * V
    extended = length + 2 * WIDTH
    lane = lanes_of((8, 128))
    place = lane % GROUP
    viscosity = [viscosity_ref[v] for v in range(V)]

    def spread_out(tile):
        reach = GROUP
        while reach < 128:
            tile = tile + pltpu.roll(tile, reach, axis=1)
            reach *= 2
        return tile

    shape = (128, 256)
    offset = lax.broadcasted_iota(jnp.int32, shape, 0) - lax.broadcasted_iota(
        jnp.int32, shape, 1
    )
    offset_column = lax.broadcasted_iota(jnp.int32, shape, 1)
    band = jnp.zeros(shape, jnp.float32)
    for gap, odd_part, even_part in ((1, 8.0, 16.0), (-1, -8.0, 16.0), (2, -1.0, -1.0), (-2, 1.0, -1.0)):
        band = jnp.where((offset == gap) & (offset_column < 128), odd_part, band)
        band = jnp.where((offset + 128 == gap) & (offset_column >= 128), even_part, band)
    for part in range(SPLIT):
        band_ref[pl.ds(128 * part, 128), :] = band.astype(jnp.bfloat16)

    @pl.loop(0, planes // 8)
    def _(block):
        for inner in range(8):
            plane = block * 8 + inner
            for source, row, target in chunks(length):
                if source == 1:
                    value = field_ref[turn * planes + plane, pl.ds(row, 8), :]
                else:
                    ref = low_ref if source == 0 else high_ref
                    value = ref[pl.ds(plane * WIDTH + row, 8), :]
                now_ref[plane, pl.ds(target, 8), :] = value

    packed = left_ref.shape[0]
    for side, own_ref in ((0, left_ref), (1, right_ref)):

        @pl.loop(0, slots + packed - PARTS * slots)
        def _(slot):
            place_in = jnp.where(slot < slots, slot + turn * slots, slot + (PARTS - 1) * slots)
            for source, row, target in chunks(length):
                if source == 1:
                    value = own_ref[place_in, pl.ds(row, 8), :]
                else:
                    ref = rim_low_ref if source == 0 else rim_high_ref
                    value = ref[pl.ds((side * packed + place_in) * WIDTH + row, 8), :]
                now_rim_ref[side, slot, pl.ds(target, 8), :] = value

    for source, row, target in chunks(length):
        raw = [
            coefficient(
                plane, source, row, planes, coupling_ref, axial_ref, radial_ref, first_low_ref, first_high_ref
            )
            for plane in range(PLANES)
        ]
        for index, value in enumerate(weights_of(raw, viscosity)):
            if index % (V + 8) < V + 4:
                weight_ref[0, index, pl.ds(target, 8), :] = value
        near = (lane >= WIDTH - 2) & (lane < WIDTH + 2)
        edge_speed, edge_inside = [
            spread_out(jnp.where(near, pltpu.roll(raw[plane], WIDTH, axis=1), 0.0))
            for plane in (V * V + 1, V * V + 2)
        ]
        edge_speed = edge_speed * (-TIME_STEP / 12.0)
        keeps = (
            place == WIDTH - 1,
            place == WIDTH,
            (place == WIDTH - 2) | (place == WIDTH - 1),
            (place == WIDTH) | (place == WIDTH + 1),
        )
        for v in range(V):
            spread = edge_inside * (viscosity[v] * (TIME_STEP / 12.0))
            for kind, value in enumerate(neighbours(spread, edge_speed)):
                edge_ref[v * 4 + kind, pl.ds(target, 8), :] = jnp.where(keeps[kind], value, 0.0)
        radial = raw[V * V + 1] * (-TIME_STEP / 12.0)
        weight_ref[0, V + 4, pl.ds(target, 8), :] = radial
        for v in range(V):
            weight_ref[0, v * (V + 8) + V + 5, pl.ds(target, 8), :] = raw[V * V + 2] * (
                viscosity[v] * (TIME_STEP / 12.0)
            )

    @pl.loop(0, extended // 8)
    def _(block):
        start = pl.multiple_of(block * 8, 8)
        for side in range(2):
            raw = []
            for plane in range(PLANES):
                tile = now_rim_ref[side, slots + plane // PER, pl.ds(start, 8), :]
                tile = pltpu.roll(tile, (128 - GROUP * (plane % PER)) % 128, axis=1)
                raw.append(spread_out(jnp.where(lane < GROUP, tile, 0.0)))
            for index, value in enumerate(weights_of(raw, viscosity)):
                weight_ref[1 + side, index, pl.ds(start, 8), :] = value

    def euler(v, kind, start, count, centers, vertical, sideways):
        def weight(index):
            return weight_ref[kind, v * (V + 8) + index, pl.ds(start, 8), :]

        totals = None
        for w in range(V):
            factor = weight(w)
            terms = [factor * centers[i][w] for i in range(count)]
            totals = terms if totals is None else [a + b for a, b in zip(totals, terms)]
        for index, step in enumerate((1, -1, 2, -2)):
            factor = weight(V + index)
            totals = [totals[i] + factor * vertical(i, step) for i in range(count)]
        if kind > 0:
            for index, step in enumerate((1, -1, 2, -2)):
                factor = weight(V + 4 + index)
                totals = [totals[i] + factor * sideways(i, step) for i in range(count)]
            return totals
        speed, spread = weight_ref[0, V + 4, pl.ds(start, 8), :], weight(V + 5)
        for i in range(count):
            one, two, rim = sideways(i, 0)
            totals[i] = ((totals[i] + rim) + speed * one) + spread * two
        return totals

    for section in range(1, SECTIONS + 1):
        odd = section % 2 == 1
        last = section == SECTIONS
        source, source_rim = (now_ref, now_rim_ref) if odd else (middle_ref, middle_rim_ref)
        target, target_rim = (middle_ref, middle_rim_ref) if odd else (now_ref, now_rim_ref)
        first = 2 * section
        blocks = -(-(extended - 2 * first) // 8)
        low_row, high_row = first // 8 * 8, -(-(extended - first) // 8) * 8

        @pl.loop(0, planes // BATCH)
        def _(batch):
            here = pl.ds(batch * BATCH, BATCH)
            rest = source[here, low_row:high_row, :].reshape(BATCH * (high_row - low_row), 128)
            halves = []
            for part in range(SPLIT):
                halves.append(rest.astype(jnp.bfloat16))
                if part < SPLIT - 1:
                    rest = rest - halves[-1].astype(jnp.float32)
            both = jnp.dot(
                jnp.concatenate(halves, axis=1), band_ref[...], preferred_element_type=jnp.float32
            )
            first_ref[here, low_row:high_row, :] = both[:, :128].reshape(BATCH, -1, 128)
            second_ref[here, low_row:high_row, :] = both[:, 128:].reshape(BATCH, -1, 128)

        @pl.loop(0, groups * blocks)
        def _(index):
            group, block = index // blocks, index % blocks
            start = first + block * 8
            joints = []
            for v in range(V):
                slot = group * V + v
                own = None
                for j in range(PER):
                    tile = source[(group * PER + j) * V + v, pl.ds(start, 8), :]
                    tile = pltpu.roll(tile, (GROUP * j + WIDTH) % 128, axis=1)
                    own = tile if own is None else jnp.where(lane >= GROUP * j, tile, own)
                left = source_rim[0, slot, pl.ds(start, 8), :]
                right = source_rim[1, slot, pl.ds(start, 8), :]
                inner = (place == WIDTH) | (place == WIDTH + 1)
                joint = jnp.where(inner, pltpu.roll(right, WIDTH - 2, axis=1), left)
                joints.append(
                    sum(
                        edge_ref[v * 4 + index, pl.ds(start, 8), :]
                        * pltpu.roll(joint, (128 - step) % 128, axis=1)
                        for index, step in enumerate((1, -1, 2, -2))
                    )
                )
                if not last:
                    source_rim[0, slot, pl.ds(start, 8), :] = jnp.where(inner, own, left)
                    source_rim[1, slot, pl.ds(start, 8), :] = jnp.where(
                        place < 2, pltpu.roll(own, 128 - (WIDTH - 2), axis=1), right
                    )

            if not last:
                for side in range(2):
                    slot = group * V
                    centers = [
                        [source_rim[side, slot + w, pl.ds(start, 8), :] for w in range(V)]
                    ]
                    for v in range(V):
                        (value,) = euler(
                            v,
                            1 + side,
                            start,
                            1,
                            centers,
                            lambda i, step: source_rim[side, slot + v, pl.ds(start + step, 8), :],
                            lambda i, step: pltpu.roll(centers[0][v], (128 - step) % 128, axis=1),
                        )
                        if not odd:
                            value = 0.5 * (value + target_rim[side, slot + v, pl.ds(start, 8), :])
                        target_rim[side, slot + v, pl.ds(start, 8), :] = value

            for part in range(PER // TOGETHER):
                bases = [(group * PER + part * TOGETHER + i) * V for i in range(TOGETHER)]
                centers = [
                    [source[base + w, pl.ds(start, 8), :] for w in range(V)] for base in bases
                ]
                for v in range(V):
                    rims = [
                        pltpu.roll(
                            joints[v],
                            (256 - WIDTH - GROUP * (part * TOGETHER + i)) % 128,
                            axis=1,
                        )
                        for i in range(TOGETHER)
                    ]
                    edge = (lane < 2) | (lane >= 126)

                    def sideways(i, step):
                        plane = bases[i] + v
                        return (
                            first_ref[plane, pl.ds(start, 8), :],
                            second_ref[plane, pl.ds(start, 8), :],
                            jnp.where(edge, rims[i], 0.0),
                        )

                    values = euler(
                        v,
                        0,
                        start,
                        TOGETHER,
                        centers,
                        lambda i, step: source[bases[i] + v, pl.ds(start + step, 8), :],
                        sideways,
                    )
                    for i in range(TOGETHER):
                        value = values[i]
                        if not odd:
                            value = 0.5 * (value + target[bases[i] + v, pl.ds(start, 8), :])
                        if last:
                            out_ref[bases[i] + v, pl.ds(start - WIDTH, 8), :] = value
                        else:
                            target[bases[i] + v, pl.ds(start, 8), :] = value


TOGETHER = 8
SPLIT = 2
BATCH = 80


def factor_kernel(parts_ref, factor_ref, inverse_ref, *, rows_all):
    total = jnp.sum(parts_ref[...], axis=0) * (1.0 / rows_all)
    order = factor_ref.shape[0]
    lane = lax.broadcasted_iota(jnp.int32, (order, 128), 1)
    row = lax.broadcasted_iota(jnp.int32, (order, 128), 0)
    pieces = [total] + [pltpu.roll(total, 128 - 32 * i, axis=1) for i in range(1, 4)]
    work = jnp.concatenate(pieces, axis=0)
    work = jnp.where(lane < order, work, jnp.where(lane == row + order, 1.0, 0.0))
    for j in range(order - 1):
        pivot_row = work[j : j + 1, :]
        scale = pivot_row / pivot_row[:, j : j + 1]
        column = jnp.where(row > j, jnp.broadcast_to(work[:, j : j + 1], work.shape), 0.0)
        work = work - column * scale
    diagonal = jnp.sum(jnp.where(lane == row, work, 0.0), axis=1, keepdims=True)
    work = work / jnp.sqrt(diagonal)
    factor_ref[...] = jnp.where(lane >= row, work, 0.0)[:, :order]
    inverse_ref[...] = jnp.where(lane <= row, pltpu.roll(work, 128 - order, axis=1), 0.0)[:, :order]


def factor_and_inverse(parts, order, rows_all):
    square = jax.ShapeDtypeStruct((order, order), jnp.float32)
    return pl.pallas_call(
        functools.partial(factor_kernel, rows_all=rows_all),
        out_shape=(square, square),
        name="factor",
    )(parts)


def shape_of(*dims):
    return jax.ShapeDtypeStruct(dims, jnp.float32)


def shifted(block, axis, step):
    size = lax.axis_size(axis)
    return lax.ppermute(
        block, axis, [(i, i + step) for i in range(size) if 0 <= i + step < size]
    )


def steps_call(part, before, viscosity, local, *received):
    planes, length, columns = local[0].shape
    rows = length + 2 * WIDTH + 8
    share = planes // PARTS
    rim = (2, received[4].shape[0] - (PARTS - 1) * share // PER, rows, columns)
    chained = [] if before is None else [before]
    return pl.pallas_call(
        functools.partial(steps_kernel, turn=part),
        grid=(1,),
        in_specs=[pl.BlockSpec(memory_space=pltpu.SMEM)]
        + whole(12)
        + [pl.BlockSpec(memory_space=pl.ANY) for _ in chained],
        out_specs=pl.BlockSpec((share, length, columns), lambda i: (part, 0, 0)),
        out_shape=shape_of(planes, length, columns),
        input_output_aliases={13: 0} if chained else {},
        scratch_shapes=[
            pltpu.VMEM((share, rows, columns), jnp.float32),
            pltpu.VMEM((share, rows, columns), jnp.float32),
            pltpu.VMEM(rim, jnp.float32),
            pltpu.VMEM(rim, jnp.float32),
            pltpu.VMEM((3, WEIGHTS, rows, columns), jnp.float32),
            pltpu.VMEM((4 * V, rows, columns), jnp.float32),
            pltpu.VMEM((share, rows, columns), jnp.float32),
            pltpu.VMEM((share, rows, columns), jnp.float32),
            pltpu.VMEM((SPLIT * columns, 2 * columns), jnp.bfloat16),
        ],
        compiler_params=pltpu.CompilerParams(vmem_limit_bytes=VMEM_LIMIT),
        name=f"steps_{part}",
    )(viscosity, *local, *received, *chained)


def per_device(forcing, vel_axial, vel_radial, coupling, viscosity):
    vectors, variables, length, columns = forcing.shape
    planes = vectors * variables
    field = forcing.reshape(planes, length, columns)
    local = (field, coupling.reshape(V * V, length, columns), vel_axial, vel_radial)
    params = pltpu.CompilerParams(vmem_limit_bytes=VMEM_LIMIT)

    def packed(part, *after):
        share = planes // PARTS
        strip = shape_of((share + (PLANES if part == 0 else 0)) * WIDTH, columns)
        return pl.pallas_call(
            functools.partial(pack_axial_kernel, begin=part * share, end=(part + 1) * share),
            in_specs=whole(4) + [pl.BlockSpec(memory_space=pl.ANY) for _ in after],
            out_specs=whole(2),
            out_shape=(strip, strip),
            compiler_params=params,
            name=f"pack_axial_{part}",
        )(*local, *after)

    up, down = packed(0)
    halos = [(shifted(up, "ax", 1), shifted(down, "ax", -1))]

    rim = shape_of(planes // PER + -(-PLANES // PER), length, columns)
    to_right, to_left = pl.pallas_call(
        pack_radial_kernel,
        in_specs=whole(4),
        out_specs=whole(2),
        out_shape=(rim, rim),
        compiler_params=params,
        name="pack_radial",
    )(*local)
    left = shifted(to_right, "rad", 1)
    right = shifted(to_left, "rad", -1)

    corner = shape_of(2 * rim.shape[0] * WIDTH, columns)
    rim_up, rim_down, corners_packed = pl.pallas_call(
        pack_corner_kernel,
        in_specs=whole(2),
        out_specs=whole(3),
        out_shape=(corner, corner, shape_of(8, columns)),
        compiler_params=params,
        name="pack_corner",
    )(left, right)
    rim_low = shifted(rim_up, "ax", 1)
    rim_high = shifted(rim_down, "ax", -1)
    response = None
    for part in range(1, PARTS):
        up, down = packed(part, corners_packed)
        halos.append((shifted(up, "ax", 1), shifted(down, "ax", -1)))
    for part in range(PARTS):
        response = steps_call(
            part, response, viscosity, local, *halos[part], *halos[0], left, right, rim_low, rim_high
        )

    flattened = response.reshape(vectors, variables * length * columns)
    devices = lax.axis_size("ax") * lax.axis_size("rad")
    rows_all = variables * length * columns * devices
    local_gram = jnp.dot(flattened, flattened.T, precision=lax.Precision.HIGHEST)
    packed = jnp.concatenate([local_gram[8 * i : 8 * i + 8] for i in range(4)], axis=1)
    copies = jnp.broadcast_to(packed, (devices, 8, 128))
    parts = lax.all_to_all(copies, ("ax", "rad"), 0, 0)
    upper_factor, lower_inverse = factor_and_inverse(parts, vectors, rows_all)
    basis = jnp.dot(lower_inverse, flattened, precision=lax.Precision.HIGHEST).reshape(forcing.shape)
    return (basis, upper_factor)


def solution(mesh):
    return jax.shard_map(
        per_device,
        mesh=mesh,
        in_specs=(
            P(None, None, "ax", "rad"),
            P("ax", "rad"),
            P("ax", "rad"),
            P(None, None, "ax", "rad"),
            P(),
        ),
        out_specs=(P(None, None, "ax", "rad"), P()),
        check_vma=False,
    )
```

```python
import functools

import jax
import jax.numpy as jnp
from jax import lax
from jax.experimental import pallas as pl
from jax.experimental.pallas import tpu as pltpu
from jax.sharding import PartitionSpec as P

STEPS = 3
TIME_STEP = 0.8
SECTIONS = 2 * STEPS
WIDTH = 2 * SECTIONS
V = 5
GROUP = 16
PER = 128 // GROUP
PLANES = V * V + 3
WEIGHTS = V * (V + 8)
VMEM_LIMIT = 56 << 20


def whole(count):
    return [pl.BlockSpec(memory_space=pltpu.VMEM) for _ in range(count)]


def lanes_of(shape):
    return lax.broadcasted_iota(jnp.int32, shape, 1)


def pack_axial_kernel(field_ref, coupling_ref, axial_ref, radial_ref, up_ref, down_ref):
    planes, length, _ = field_ref.shape
    low = length - WIDTH

    def put(slot, read):
        base = slot * WIDTH
        for start in range(0, WIDTH, 8):
            size = min(8, WIDTH - start)
            up_ref[pl.ds(base + start, size), :] = read(low + start, size)
            down_ref[pl.ds(base + start, size), :] = read(start, size)

    @pl.loop(0, planes // 8)
    def _(block):
        for inner in range(8):
            plane = block * 8 + inner
            put(plane, lambda start, size: field_ref[plane, pl.ds(start, size), :])

    for plane in range(V * V):
        put(planes + plane, lambda start, size: coupling_ref[plane, pl.ds(start, size), :])
    put(planes + V * V, lambda start, size: axial_ref[pl.ds(start, size), :])
    put(planes + V * V + 1, lambda start, size: radial_ref[pl.ds(start, size), :])
    put(planes + V * V + 2, lambda start, size: jnp.ones((size, 128), jnp.float32))


def chunks(length):
    rim = sorted({*range(0, WIDTH - 7, 8), WIDTH - 8})
    return (
        [(0, row, row) for row in rim]
        + [(1, row, WIDTH + row) for row in range(0, length, 8)]
        + [(2, row, WIDTH + length + row) for row in rim]
    )


def coefficient(plane, source, row, planes, coupling_ref, axial_ref, radial_ref, low_ref, high_ref):
    if source != 1:
        ref = low_ref if source == 0 else high_ref
        return ref[pl.ds((planes + plane) * WIDTH + row, 8), :]
    if plane < V * V:
        return coupling_ref[plane, pl.ds(row, 8), :]
    if plane == V * V + 2:
        return jnp.ones((8, 128), jnp.float32)
    return (axial_ref if plane == V * V else radial_ref)[pl.ds(row, 8), :]


def pack_radial_kernel(field_ref, coupling_ref, axial_ref, radial_ref, right_ref, left_ref):
    planes, length, _ = field_ref.shape
    groups = planes // (V * PER)
    lane = lanes_of((8, 128))

    def merge(tiles, offset):
        merged = pltpu.roll(tiles[0], offset, axis=1)
        for j in range(1, len(tiles)):
            merged = jnp.where(
                lane >= GROUP * j, pltpu.roll(tiles[j], (GROUP * j + offset) % 128, axis=1), merged
            )
        return merged

    def put(slot, row, tiles):
        right_ref[slot, pl.ds(row, 8), :] = merge(tiles, WIDTH)
        left_ref[slot, pl.ds(row, 8), :] = merge(tiles, 2)

    @pl.loop(0, groups)
    def _(group):
        for v in range(V):
            for row in range(0, length, 8):
                put(
                    group * V + v,
                    row,
                    [field_ref[(group * PER + j) * V + v, pl.ds(row, 8), :] for j in range(PER)],
                )

    for slot in range(-(-PLANES // PER)):
        for row in range(0, length, 8):
            tiles = [
                coefficient(plane, 1, row, planes, coupling_ref, axial_ref, radial_ref, None, None)
                for plane in range(slot * PER, min(PLANES, (slot + 1) * PER))
            ]
            put(groups * V + slot, row, tiles)


def pack_corner_kernel(left_ref, right_ref, up_ref, down_ref):
    slots, length, _ = left_ref.shape
    low = length - WIDTH
    for side, ref in ((0, left_ref), (1, right_ref)):
        for slot in range(slots):
            base = (side * slots + slot) * WIDTH
            for start in range(0, WIDTH, 8):
                size = min(8, WIDTH - start)
                up_ref[base + start : base + start + size, :] = ref[
                    slot, low + start : low + start + size, :
                ]
                down_ref[base + start : base + start + size, :] = ref[slot, start : start + size, :]


def neighbours(spread, speed):
    return (
        16.0 * spread + 8.0 * speed,
        16.0 * spread - 8.0 * speed,
        -spread - speed,
        speed - spread,
    )


def weights_of(raw, viscosity):
    axial = raw[V * V] * (-TIME_STEP / 12.0)
    radial = raw[V * V + 1] * (-TIME_STEP / 12.0)
    inside = raw[V * V + 2]
    found = []
    for v in range(V):
        spread = inside * (viscosity[v] * (TIME_STEP / 12.0))
        for w in range(V):
            value = raw[v * V + w] * TIME_STEP
            found.append(value + (1.0 - 60.0 * spread) if v == w else value)
        for speed in (axial, radial):
            found.extend(neighbours(spread, speed))
    return found


def steps_kernel(
    viscosity_ref,
    field_ref,
    coupling_ref,
    axial_ref,
    radial_ref,
    low_ref,
    high_ref,
    left_ref,
    right_ref,
    rim_low_ref,
    rim_high_ref,
    out_ref,
    now_ref,
    middle_ref,
    now_rim_ref,
    middle_rim_ref,
    weight_ref,
    edge_ref,
    first_ref,
    second_ref,
    band_ref,
):
    planes, length, _ = field_ref.shape
    vectors = planes // V
    groups = vectors // PER
    slots = groups * V
    extended = length + 2 * WIDTH
    lane = lanes_of((8, 128))
    place = lane % GROUP
    viscosity = [viscosity_ref[v] for v in range(V)]

    def spread_out(tile):
        reach = GROUP
        while reach < 128:
            tile = tile + pltpu.roll(tile, reach, axis=1)
            reach *= 2
        return tile

    shape = (128, 256)
    offset = lax.broadcasted_iota(jnp.int32, shape, 0) - lax.broadcasted_iota(
        jnp.int32, shape, 1
    )
    offset_column = lax.broadcasted_iota(jnp.int32, shape, 1)
    band = jnp.zeros(shape, jnp.float32)
    for gap, odd_part, even_part in ((1, 8.0, 16.0), (-1, -8.0, 16.0), (2, -1.0, -1.0), (-2, 1.0, -1.0)):
        band = jnp.where((offset == gap) & (offset_column < 128), odd_part, band)
        band = jnp.where((offset + 128 == gap) & (offset_column >= 128), even_part, band)
    for part in range(SPLIT):
        band_ref[pl.ds(128 * part, 128), :] = band.astype(jnp.bfloat16)

    @pl.loop(0, planes // 8)
    def _(block):
        for inner in range(8):
            plane = block * 8 + inner
            for source, row, target in chunks(length):
                if source == 1:
                    value = field_ref[plane, pl.ds(row, 8), :]
                else:
                    ref = low_ref if source == 0 else high_ref
                    value = ref[pl.ds(plane * WIDTH + row, 8), :]
                now_ref[plane, pl.ds(target, 8), :] = value

    packed = left_ref.shape[0]
    for side, own_ref in ((0, left_ref), (1, right_ref)):

        @pl.loop(0, packed)
        def _(slot):
            for source, row, target in chunks(length):
                if source == 1:
                    value = own_ref[slot, pl.ds(row, 8), :]
                else:
                    ref = rim_low_ref if source == 0 else rim_high_ref
                    value = ref[pl.ds((side * packed + slot) * WIDTH + row, 8), :]
                now_rim_ref[side, slot, pl.ds(target, 8), :] = value

    for source, row, target in chunks(length):
        raw = [
            coefficient(
                plane, source, row, planes, coupling_ref, axial_ref, radial_ref, low_ref, high_ref
            )
            for plane in range(PLANES)
        ]
        for index, value in enumerate(weights_of(raw, viscosity)):
            if index % (V + 8) < V + 4:
                weight_ref[0, index, pl.ds(target, 8), :] = value
        near = (lane >= WIDTH - 2) & (lane < WIDTH + 2)
        edge_speed, edge_inside = [
            spread_out(jnp.where(near, pltpu.roll(raw[plane], WIDTH, axis=1), 0.0))
            for plane in (V * V + 1, V * V + 2)
        ]
        edge_speed = edge_speed * (-TIME_STEP / 12.0)
        keeps = (
            place == WIDTH - 1,
            place == WIDTH,
            (place == WIDTH - 2) | (place == WIDTH - 1),
            (place == WIDTH) | (place == WIDTH + 1),
        )
        for v in range(V):
            spread = edge_inside * (viscosity[v] * (TIME_STEP / 12.0))
            for kind, value in enumerate(neighbours(spread, edge_speed)):
                edge_ref[v * 4 + kind, pl.ds(target, 8), :] = jnp.where(keeps[kind], value, 0.0)
        radial = raw[V * V + 1] * (-TIME_STEP / 12.0)
        weight_ref[0, V + 4, pl.ds(target, 8), :] = radial
        for v in range(V):
            weight_ref[0, v * (V + 8) + V + 5, pl.ds(target, 8), :] = raw[V * V + 2] * (
                viscosity[v] * (TIME_STEP / 12.0)
            )

    @pl.loop(0, extended // 8)
    def _(block):
        start = pl.multiple_of(block * 8, 8)
        for side in range(2):
            raw = []
            for plane in range(PLANES):
                tile = now_rim_ref[side, slots + plane // PER, pl.ds(start, 8), :]
                tile = pltpu.roll(tile, (128 - GROUP * (plane % PER)) % 128, axis=1)
                raw.append(spread_out(jnp.where(lane < GROUP, tile, 0.0)))
            for index, value in enumerate(weights_of(raw, viscosity)):
                weight_ref[1 + side, index, pl.ds(start, 8), :] = value

    def euler(v, kind, start, count, centers, vertical, sideways):
        def weight(index):
            return weight_ref[kind, v * (V + 8) + index, pl.ds(start, 8), :]

        totals = None
        for w in range(V):
            factor = weight(w)
            terms = [factor * centers[i][w] for i in range(count)]
            totals = terms if totals is None else [a + b for a, b in zip(totals, terms)]
        for index, step in enumerate((1, -1, 2, -2)):
            factor = weight(V + index)
            totals = [totals[i] + factor * vertical(i, step) for i in range(count)]
        if kind > 0:
            for index, step in enumerate((1, -1, 2, -2)):
                factor = weight(V + 4 + index)
                totals = [totals[i] + factor * sideways(i, step) for i in range(count)]
            return totals
        speed, spread = weight_ref[0, V + 4, pl.ds(start, 8), :], weight(V + 5)
        for i in range(count):
            one, two, rim = sideways(i, 0)
            totals[i] = ((totals[i] + rim) + speed * one) + spread * two
        return totals

    for section in range(1, SECTIONS + 1):
        odd = section % 2 == 1
        last = section == SECTIONS
        source, source_rim = (now_ref, now_rim_ref) if odd else (middle_ref, middle_rim_ref)
        target, target_rim = (middle_ref, middle_rim_ref) if odd else (now_ref, now_rim_ref)
        first = 2 * section
        blocks = -(-(extended - 2 * first) // 8)
        low_row, high_row = first // 8 * 8, -(-(extended - first) // 8) * 8

        @pl.loop(0, planes // BATCH)
        def _(batch):
            here = pl.ds(batch * BATCH, BATCH)
            rest = source[here, low_row:high_row, :].reshape(BATCH * (high_row - low_row), 128)
            halves = []
            for part in range(SPLIT):
                halves.append(rest.astype(jnp.bfloat16))
                if part < SPLIT - 1:
                    rest = rest - halves[-1].astype(jnp.float32)
            both = jnp.dot(
                jnp.concatenate(halves, axis=1), band_ref[...], preferred_element_type=jnp.float32
            )
            first_ref[here, low_row:high_row, :] = both[:, :128].reshape(BATCH, -1, 128)
            second_ref[here, low_row:high_row, :] = both[:, 128:].reshape(BATCH, -1, 128)

        @pl.loop(0, groups * blocks)
        def _(index):
            group, block = index // blocks, index % blocks
            start = first + block * 8
            joints = []
            for v in range(V):
                slot = group * V + v
                own = None
                for j in range(PER):
                    tile = source[(group * PER + j) * V + v, pl.ds(start, 8), :]
                    tile = pltpu.roll(tile, (GROUP * j + WIDTH) % 128, axis=1)
                    own = tile if own is None else jnp.where(lane >= GROUP * j, tile, own)
                left = source_rim[0, slot, pl.ds(start, 8), :]
                right = source_rim[1, slot, pl.ds(start, 8), :]
                inner = (place == WIDTH) | (place == WIDTH + 1)
                joint = jnp.where(inner, pltpu.roll(right, WIDTH - 2, axis=1), left)
                joints.append(
                    sum(
                        edge_ref[v * 4 + index, pl.ds(start, 8), :]
                        * pltpu.roll(joint, (128 - step) % 128, axis=1)
                        for index, step in enumerate((1, -1, 2, -2))
                    )
                )
                if not last:
                    source_rim[0, slot, pl.ds(start, 8), :] = jnp.where(inner, own, left)
                    source_rim[1, slot, pl.ds(start, 8), :] = jnp.where(
                        place < 2, pltpu.roll(own, 128 - (WIDTH - 2), axis=1), right
                    )

            if not last:
                for side in range(2):
                    slot = group * V
                    centers = [
                        [source_rim[side, slot + w, pl.ds(start, 8), :] for w in range(V)]
                    ]
                    for v in range(V):
                        (value,) = euler(
                            v,
                            1 + side,
                            start,
                            1,
                            centers,
                            lambda i, step: source_rim[side, slot + v, pl.ds(start + step, 8), :],
                            lambda i, step: pltpu.roll(centers[0][v], (128 - step) % 128, axis=1),
                        )
                        if not odd:
                            value = 0.5 * (value + target_rim[side, slot + v, pl.ds(start, 8), :])
                        target_rim[side, slot + v, pl.ds(start, 8), :] = value

            for part in range(PER // TOGETHER):
                bases = [(group * PER + part * TOGETHER + i) * V for i in range(TOGETHER)]
                centers = [
                    [source[base + w, pl.ds(start, 8), :] for w in range(V)] for base in bases
                ]
                for v in range(V):
                    rims = [
                        pltpu.roll(
                            joints[v],
                            (256 - WIDTH - GROUP * (part * TOGETHER + i)) % 128,
                            axis=1,
                        )
                        for i in range(TOGETHER)
                    ]
                    edge = (lane < 2) | (lane >= 126)

                    def sideways(i, step):
                        plane = bases[i] + v
                        return (
                            first_ref[plane, pl.ds(start, 8), :],
                            second_ref[plane, pl.ds(start, 8), :],
                            jnp.where(edge, rims[i], 0.0),
                        )

                    values = euler(
                        v,
                        0,
                        start,
                        TOGETHER,
                        centers,
                        lambda i, step: source[bases[i] + v, pl.ds(start + step, 8), :],
                        sideways,
                    )
                    for i in range(TOGETHER):
                        value = values[i]
                        if not odd:
                            value = 0.5 * (value + target[bases[i] + v, pl.ds(start, 8), :])
                        if last:
                            out_ref[bases[i] + v, pl.ds(start - WIDTH, 8), :] = value
                        else:
                            target[bases[i] + v, pl.ds(start, 8), :] = value


TOGETHER = 8
SPLIT = 2
BATCH = 80


def factor_kernel(parts_ref, factor_ref, inverse_ref, *, rows_all):
    total = jnp.sum(parts_ref[...], axis=0) * (1.0 / rows_all)
    order = factor_ref.shape[0]
    lane = lax.broadcasted_iota(jnp.int32, (order, 128), 1)
    row = lax.broadcasted_iota(jnp.int32, (order, 128), 0)
    pieces = [total] + [pltpu.roll(total, 128 - 32 * i, axis=1) for i in range(1, 4)]
    work = jnp.concatenate(pieces, axis=0)
    work = jnp.where(lane < order, work, jnp.where(lane == row + order, 1.0, 0.0))
    for j in range(order - 1):
        pivot_row = work[j : j + 1, :]
        scale = pivot_row / pivot_row[:, j : j + 1]
        column = jnp.where(row > j, jnp.broadcast_to(work[:, j : j + 1], work.shape), 0.0)
        work = work - column * scale
    diagonal = jnp.sum(jnp.where(lane == row, work, 0.0), axis=1, keepdims=True)
    work = work / jnp.sqrt(diagonal)
    factor_ref[...] = jnp.where(lane >= row, work, 0.0)[:, :order]
    inverse_ref[...] = jnp.where(lane <= row, pltpu.roll(work, 128 - order, axis=1), 0.0)[:, :order]


def factor_and_inverse(parts, order, rows_all):
    square = jax.ShapeDtypeStruct((order, order), jnp.float32)
    return pl.pallas_call(
        functools.partial(factor_kernel, rows_all=rows_all),
        out_shape=(square, square),
        name="factor",
    )(parts)


def shape_of(*dims):
    return jax.ShapeDtypeStruct(dims, jnp.float32)


def shifted(block, axis, step):
    size = lax.axis_size(axis)
    return lax.ppermute(
        block, axis, [(i, i + step) for i in range(size) if 0 <= i + step < size]
    )


def steps_call(viscosity, local, *received):
    planes, length, columns = local[0].shape
    rows = length + 2 * WIDTH + 8
    return pl.pallas_call(
        steps_kernel,
        in_specs=[pl.BlockSpec(memory_space=pltpu.SMEM)] + whole(10),
        out_specs=whole(1)[0],
        out_shape=shape_of(planes, length, columns),
        scratch_shapes=[
            pltpu.VMEM((planes, rows, columns), jnp.float32),
            pltpu.VMEM((planes, rows, columns), jnp.float32),
            pltpu.VMEM((2, received[2].shape[0], rows, columns), jnp.float32),
            pltpu.VMEM((2, planes // PER, rows, columns), jnp.float32),
            pltpu.VMEM((3, WEIGHTS, rows, columns), jnp.float32),
            pltpu.VMEM((4 * V, rows, columns), jnp.float32),
            pltpu.VMEM((planes, rows, columns), jnp.float32),
            pltpu.VMEM((planes, rows, columns), jnp.float32),
            pltpu.VMEM((SPLIT * columns, 2 * columns), jnp.bfloat16),
        ],
        compiler_params=pltpu.CompilerParams(vmem_limit_bytes=VMEM_LIMIT),
        name="steps",
    )(viscosity, *local, *received)


def per_device(forcing, vel_axial, vel_radial, coupling, viscosity):
    vectors, variables, length, columns = forcing.shape
    planes = vectors * variables
    field = forcing.reshape(planes, length, columns)
    local = (field, coupling.reshape(V * V, length, columns), vel_axial, vel_radial)
    params = pltpu.CompilerParams(vmem_limit_bytes=VMEM_LIMIT)

    strip = shape_of((planes + PLANES) * WIDTH, columns)
    up, down = pl.pallas_call(
        pack_axial_kernel,
        in_specs=whole(4),
        out_specs=whole(2),
        out_shape=(strip, strip),
        compiler_params=params,
        name="pack_axial",
    )(*local)
    low = shifted(up, "ax", 1)
    high = shifted(down, "ax", -1)

    rim = shape_of(planes // PER + -(-PLANES // PER), length, columns)
    to_right, to_left = pl.pallas_call(
        pack_radial_kernel,
        in_specs=whole(4),
        out_specs=whole(2),
        out_shape=(rim, rim),
        compiler_params=params,
        name="pack_radial",
    )(*local)
    left = shifted(to_right, "rad", 1)
    right = shifted(to_left, "rad", -1)

    corner = shape_of(2 * rim.shape[0] * WIDTH, columns)
    rim_up, rim_down = pl.pallas_call(
        pack_corner_kernel,
        in_specs=whole(2),
        out_specs=whole(2),
        out_shape=(corner, corner),
        compiler_params=params,
        name="pack_corner",
    )(left, right)
    rim_low = shifted(rim_up, "ax", 1)
    rim_high = shifted(rim_down, "ax", -1)
    response = steps_call(viscosity, local, low, high, left, right, rim_low, rim_high)

    flattened = response.reshape(vectors, variables * length * columns)
    devices = lax.axis_size("ax") * lax.axis_size("rad")
    rows_all = variables * length * columns * devices
    local_gram = jnp.dot(flattened, flattened.T, precision=lax.Precision.HIGHEST)
    packed = jnp.concatenate([local_gram[8 * i : 8 * i + 8] for i in range(4)], axis=1)
    pairs = [(i, i ^ 1) for i in range(lax.axis_size("rad"))]
    packed = packed + lax.ppermute(packed, "rad", pairs)
    copies = jnp.broadcast_to(packed, (devices // 2, 8, 128))
    halves = [list(range(parity, devices, 2)) for parity in range(2)]
    parts = lax.all_to_all(copies, ("ax", "rad"), 0, 0, axis_index_groups=halves)
    upper_factor, lower_inverse = factor_and_inverse(parts, vectors, rows_all)
    basis = jnp.dot(lower_inverse, flattened, precision=lax.Precision.HIGHEST).reshape(forcing.shape)
    return (basis, upper_factor)


def solution(mesh):
    return jax.shard_map(
        per_device,
        mesh=mesh,
        in_specs=(
            P(None, None, "ax", "rad"),
            P("ax", "rad"),
            P("ax", "rad"),
            P(None, None, "ax", "rad"),
            P(),
        ),
        out_specs=(P(None, None, "ax", "rad"), P()),
        check_vma=False,
    )
```

```python
import functools

import jax
import jax.numpy as jnp
from jax import lax
from jax.experimental import pallas as pl
from jax.experimental.pallas import tpu as pltpu
from jax.sharding import PartitionSpec as P

STEPS = 3
TIME_STEP = 0.8
SECTIONS = 2 * STEPS
WIDTH = 2 * SECTIONS
V = 5
GROUP = 16
PER = 128 // GROUP
PLANES = V * V + 3
WEIGHTS = V * (V + 8)
VMEM_LIMIT = 56 << 20


def whole(count):
    return [pl.BlockSpec(memory_space=pltpu.VMEM) for _ in range(count)]


def lanes_of(shape):
    return lax.broadcasted_iota(jnp.int32, shape, 1)


def pack_axial_kernel(field_ref, coupling_ref, axial_ref, radial_ref, up_ref, down_ref):
    planes, length, _ = field_ref.shape
    low = length - WIDTH

    def put(slot, read):
        base = slot * WIDTH
        for start in range(0, WIDTH, 8):
            size = min(8, WIDTH - start)
            up_ref[pl.ds(base + start, size), :] = read(low + start, size)
            down_ref[pl.ds(base + start, size), :] = read(start, size)

    @pl.loop(0, planes // 8)
    def _(block):
        for inner in range(8):
            plane = block * 8 + inner
            put(plane, lambda start, size: field_ref[plane, pl.ds(start, size), :])

    for plane in range(V * V):
        put(planes + plane, lambda start, size: coupling_ref[plane, pl.ds(start, size), :])
    put(planes + V * V, lambda start, size: axial_ref[pl.ds(start, size), :])
    put(planes + V * V + 1, lambda start, size: radial_ref[pl.ds(start, size), :])
    put(planes + V * V + 2, lambda start, size: jnp.ones((size, 128), jnp.float32))


def chunks(length):
    rim = sorted({*range(0, WIDTH - 7, 8), WIDTH - 8})
    return (
        [(0, row, row) for row in rim]
        + [(1, row, WIDTH + row) for row in range(0, length, 8)]
        + [(2, row, WIDTH + length + row) for row in rim]
    )


def coefficient(plane, source, row, planes, coupling_ref, axial_ref, radial_ref, low_ref, high_ref):
    if source != 1:
        ref = low_ref if source == 0 else high_ref
        return ref[pl.ds((planes + plane) * WIDTH + row, 8), :]
    if plane < V * V:
        return coupling_ref[plane, pl.ds(row, 8), :]
    if plane == V * V + 2:
        return jnp.ones((8, 128), jnp.float32)
    return (axial_ref if plane == V * V else radial_ref)[pl.ds(row, 8), :]


def pack_radial_kernel(field_ref, coupling_ref, axial_ref, radial_ref, right_ref, left_ref):
    planes, length, _ = field_ref.shape
    groups = planes // (V * PER)
    lane = lanes_of((8, 128))

    def merge(tiles, offset):
        merged = pltpu.roll(tiles[0], offset, axis=1)
        for j in range(1, len(tiles)):
            merged = jnp.where(
                lane >= GROUP * j, pltpu.roll(tiles[j], (GROUP * j + offset) % 128, axis=1), merged
            )
        return merged

    def put(slot, row, tiles):
        right_ref[slot, pl.ds(row, 8), :] = merge(tiles, WIDTH)
        left_ref[slot, pl.ds(row, 8), :] = merge(tiles, 2)

    @pl.loop(0, groups)
    def _(group):
        for v in range(V):
            for row in range(0, length, 8):
                put(
                    group * V + v,
                    row,
                    [field_ref[(group * PER + j) * V + v, pl.ds(row, 8), :] for j in range(PER)],
                )

    for slot in range(-(-PLANES // PER)):
        for row in range(0, length, 8):
            tiles = [
                coefficient(plane, 1, row, planes, coupling_ref, axial_ref, radial_ref, None, None)
                for plane in range(slot * PER, min(PLANES, (slot + 1) * PER))
            ]
            put(groups * V + slot, row, tiles)


def pack_corner_kernel(left_ref, right_ref, up_ref, down_ref):
    slots, length, _ = left_ref.shape
    low = length - WIDTH
    for side, ref in ((0, left_ref), (1, right_ref)):
        for slot in range(slots):
            base = (side * slots + slot) * WIDTH
            for start in range(0, WIDTH, 8):
                size = min(8, WIDTH - start)
                up_ref[base + start : base + start + size, :] = ref[
                    slot, low + start : low + start + size, :
                ]
                down_ref[base + start : base + start + size, :] = ref[slot, start : start + size, :]


def neighbours(spread, speed):
    return (
        16.0 * spread + 8.0 * speed,
        16.0 * spread - 8.0 * speed,
        -spread - speed,
        speed - spread,
    )


def weights_of(raw, viscosity):
    axial = raw[V * V] * (-TIME_STEP / 12.0)
    radial = raw[V * V + 1] * (-TIME_STEP / 12.0)
    inside = raw[V * V + 2]
    found = []
    for v in range(V):
        spread = inside * (viscosity[v] * (TIME_STEP / 12.0))
        for w in range(V):
            value = raw[v * V + w] * TIME_STEP
            found.append(value + (1.0 - 60.0 * spread) if v == w else value)
        for speed in (axial, radial):
            found.extend(neighbours(spread, speed))
    return found


def steps_kernel(
    viscosity_ref,
    field_ref,
    coupling_ref,
    axial_ref,
    radial_ref,
    low_ref,
    high_ref,
    left_ref,
    right_ref,
    rim_low_ref,
    rim_high_ref,
    out_ref,
    now_ref,
    middle_ref,
    now_rim_ref,
    middle_rim_ref,
    weight_ref,
    edge_ref,
    first_ref,
    second_ref,
    band_ref,
):
    planes, length, _ = field_ref.shape
    vectors = planes // V
    groups = vectors // PER
    slots = groups * V
    extended = length + 2 * WIDTH
    lane = lanes_of((8, 128))
    place = lane % GROUP
    viscosity = [viscosity_ref[v] for v in range(V)]

    def spread_out(tile):
        reach = GROUP
        while reach < 128:
            tile = tile + pltpu.roll(tile, reach, axis=1)
            reach *= 2
        return tile

    shape = (128, 256)
    offset = lax.broadcasted_iota(jnp.int32, shape, 0) - lax.broadcasted_iota(
        jnp.int32, shape, 1
    )
    offset_column = lax.broadcasted_iota(jnp.int32, shape, 1)
    band = jnp.zeros(shape, jnp.float32)
    for gap, odd_part, even_part in ((1, 8.0, 16.0), (-1, -8.0, 16.0), (2, -1.0, -1.0), (-2, 1.0, -1.0)):
        band = jnp.where((offset == gap) & (offset_column < 128), odd_part, band)
        band = jnp.where((offset + 128 == gap) & (offset_column >= 128), even_part, band)
    for part in range(SPLIT):
        band_ref[pl.ds(128 * part, 128), :] = band.astype(jnp.bfloat16)

    @pl.loop(0, planes // 8)
    def _(block):
        for inner in range(8):
            plane = block * 8 + inner
            for source, row, target in chunks(length):
                if source == 1:
                    value = field_ref[plane, pl.ds(row, 8), :]
                else:
                    ref = low_ref if source == 0 else high_ref
                    value = ref[pl.ds(plane * WIDTH + row, 8), :]
                now_ref[plane, pl.ds(target, 8), :] = value

    packed = left_ref.shape[0]
    for side, own_ref in ((0, left_ref), (1, right_ref)):

        @pl.loop(0, packed)
        def _(slot):
            for source, row, target in chunks(length):
                if source == 1:
                    value = own_ref[slot, pl.ds(row, 8), :]
                else:
                    ref = rim_low_ref if source == 0 else rim_high_ref
                    value = ref[pl.ds((side * packed + slot) * WIDTH + row, 8), :]
                now_rim_ref[side, slot, pl.ds(target, 8), :] = value

    for source, row, target in chunks(length):
        raw = [
            coefficient(
                plane, source, row, planes, coupling_ref, axial_ref, radial_ref, low_ref, high_ref
            )
            for plane in range(PLANES)
        ]
        for index, value in enumerate(weights_of(raw, viscosity)):
            if index % (V + 8) < V + 4:
                weight_ref[0, index, pl.ds(target, 8), :] = value
        near = (lane >= WIDTH - 2) & (lane < WIDTH + 2)
        edge_speed, edge_inside = [
            spread_out(jnp.where(near, pltpu.roll(raw[plane], WIDTH, axis=1), 0.0))
            for plane in (V * V + 1, V * V + 2)
        ]
        edge_speed = edge_speed * (-TIME_STEP / 12.0)
        keeps = (
            place == WIDTH - 1,
            place == WIDTH,
            (place == WIDTH - 2) | (place == WIDTH - 1),
            (place == WIDTH) | (place == WIDTH + 1),
        )
        for v in range(V):
            spread = edge_inside * (viscosity[v] * (TIME_STEP / 12.0))
            for kind, value in enumerate(neighbours(spread, edge_speed)):
                edge_ref[v * 4 + kind, pl.ds(target, 8), :] = jnp.where(keeps[kind], value, 0.0)
        radial = raw[V * V + 1] * (-TIME_STEP / 12.0)
        weight_ref[0, V + 4, pl.ds(target, 8), :] = radial
        for v in range(V):
            weight_ref[0, v * (V + 8) + V + 5, pl.ds(target, 8), :] = raw[V * V + 2] * (
                viscosity[v] * (TIME_STEP / 12.0)
            )

    @pl.loop(0, extended // 8)
    def _(block):
        start = pl.multiple_of(block * 8, 8)
        for side in range(2):
            raw = []
            for plane in range(PLANES):
                tile = now_rim_ref[side, slots + plane // PER, pl.ds(start, 8), :]
                tile = pltpu.roll(tile, (128 - GROUP * (plane % PER)) % 128, axis=1)
                raw.append(spread_out(jnp.where(lane < GROUP, tile, 0.0)))
            for index, value in enumerate(weights_of(raw, viscosity)):
                weight_ref[1 + side, index, pl.ds(start, 8), :] = value

    def euler(v, kind, start, count, centers, vertical, sideways):
        def weight(index):
            return weight_ref[kind, v * (V + 8) + index, pl.ds(start, 8), :]

        totals = None
        for w in range(V):
            factor = weight(w)
            terms = [factor * centers[i][w] for i in range(count)]
            totals = terms if totals is None else [a + b for a, b in zip(totals, terms)]
        for index, step in enumerate((1, -1, 2, -2)):
            factor = weight(V + index)
            totals = [totals[i] + factor * vertical(i, step) for i in range(count)]
        if kind > 0:
            for index, step in enumerate((1, -1, 2, -2)):
                factor = weight(V + 4 + index)
                totals = [totals[i] + factor * sideways(i, step) for i in range(count)]
            return totals
        speed, spread = weight_ref[0, V + 4, pl.ds(start, 8), :], weight(V + 5)
        for i in range(count):
            one, two, rim = sideways(i, 0)
            totals[i] = ((totals[i] + rim) + speed * one) + spread * two
        return totals

    for section in range(1, SECTIONS + 1):
        odd = section % 2 == 1
        last = section == SECTIONS
        source, source_rim = (now_ref, now_rim_ref) if odd else (middle_ref, middle_rim_ref)
        target, target_rim = (middle_ref, middle_rim_ref) if odd else (now_ref, now_rim_ref)
        first = 2 * section
        blocks = -(-(extended - 2 * first) // 8)
        low_row, high_row = first // 8 * 8, -(-(extended - first) // 8) * 8

        @pl.loop(0, planes // BATCH)
        def _(batch):
            here = pl.ds(batch * BATCH, BATCH)
            rest = source[here, low_row:high_row, :].reshape(BATCH * (high_row - low_row), 128)
            halves = []
            for part in range(SPLIT):
                halves.append(rest.astype(jnp.bfloat16))
                if part < SPLIT - 1:
                    rest = rest - halves[-1].astype(jnp.float32)
            both = jnp.dot(
                jnp.concatenate(halves, axis=1), band_ref[...], preferred_element_type=jnp.float32
            )
            first_ref[here, low_row:high_row, :] = both[:, :128].reshape(BATCH, -1, 128)
            second_ref[here, low_row:high_row, :] = both[:, 128:].reshape(BATCH, -1, 128)

        @pl.loop(0, groups * blocks)
        def _(index):
            group, block = index // blocks, index % blocks
            start = first + block * 8
            joints = []
            for v in range(V):
                slot = group * V + v
                own = None
                for j in range(PER):
                    tile = source[(group * PER + j) * V + v, pl.ds(start, 8), :]
                    tile = pltpu.roll(tile, (GROUP * j + WIDTH) % 128, axis=1)
                    own = tile if own is None else jnp.where(lane >= GROUP * j, tile, own)
                left = source_rim[0, slot, pl.ds(start, 8), :]
                right = source_rim[1, slot, pl.ds(start, 8), :]
                inner = (place == WIDTH) | (place == WIDTH + 1)
                joint = jnp.where(inner, pltpu.roll(right, WIDTH - 2, axis=1), left)
                joints.append(
                    sum(
                        edge_ref[v * 4 + index, pl.ds(start, 8), :]
                        * pltpu.roll(joint, (128 - step) % 128, axis=1)
                        for index, step in enumerate((1, -1, 2, -2))
                    )
                )
                if not last:
                    source_rim[0, slot, pl.ds(start, 8), :] = jnp.where(inner, own, left)
                    source_rim[1, slot, pl.ds(start, 8), :] = jnp.where(
                        place < 2, pltpu.roll(own, 128 - (WIDTH - 2), axis=1), right
                    )

            if not last:
                for side in range(2):
                    slot = group * V
                    centers = [
                        [source_rim[side, slot + w, pl.ds(start, 8), :] for w in range(V)]
                    ]
                    for v in range(V):
                        (value,) = euler(
                            v,
                            1 + side,
                            start,
                            1,
                            centers,
                            lambda i, step: source_rim[side, slot + v, pl.ds(start + step, 8), :],
                            lambda i, step: pltpu.roll(centers[0][v], (128 - step) % 128, axis=1),
                        )
                        if not odd:
                            value = 0.5 * (value + target_rim[side, slot + v, pl.ds(start, 8), :])
                        target_rim[side, slot + v, pl.ds(start, 8), :] = value

            for part in range(PER // TOGETHER):
                bases = [(group * PER + part * TOGETHER + i) * V for i in range(TOGETHER)]
                centers = [
                    [source[base + w, pl.ds(start, 8), :] for w in range(V)] for base in bases
                ]
                for v in range(V):
                    rims = [
                        pltpu.roll(
                            joints[v],
                            (256 - WIDTH - GROUP * (part * TOGETHER + i)) % 128,
                            axis=1,
                        )
                        for i in range(TOGETHER)
                    ]
                    edge = (lane < 2) | (lane >= 126)

                    def sideways(i, step):
                        plane = bases[i] + v
                        return (
                            first_ref[plane, pl.ds(start, 8), :],
                            second_ref[plane, pl.ds(start, 8), :],
                            jnp.where(edge, rims[i], 0.0),
                        )

                    values = euler(
                        v,
                        0,
                        start,
                        TOGETHER,
                        centers,
                        lambda i, step: source[bases[i] + v, pl.ds(start + step, 8), :],
                        sideways,
                    )
                    for i in range(TOGETHER):
                        value = values[i]
                        if not odd:
                            value = 0.5 * (value + target[bases[i] + v, pl.ds(start, 8), :])
                        if last:
                            out_ref[bases[i] + v, pl.ds(start - WIDTH, 8), :] = value
                        else:
                            target[bases[i] + v, pl.ds(start, 8), :] = value


TOGETHER = 8
SPLIT = 2
BATCH = 80


def factor_kernel(parts_ref, factor_ref, inverse_ref, *, rows_all):
    total = jnp.sum(parts_ref[...], axis=0) * (1.0 / rows_all)
    order = factor_ref.shape[0]
    lane = lax.broadcasted_iota(jnp.int32, (order, 128), 1)
    row = lax.broadcasted_iota(jnp.int32, (order, 128), 0)
    pieces = [total] + [pltpu.roll(total, 128 - 32 * i, axis=1) for i in range(1, 4)]
    work = jnp.concatenate(pieces, axis=0)
    work = jnp.where(lane < order, work, jnp.where(lane == row + order, 1.0, 0.0))
    for j in range(0, order, 2):
        one, two = work[j : j + 1, :], work[j + 1 : j + 2, :]
        left, right = [jnp.broadcast_to(work[:, i : i + 1], work.shape) for i in (j, j + 1)]
        scale = one / one[:, j : j + 1]
        step = one[:, j + 1 : j + 2] / one[:, j : j + 1]
        two_cleared = two - two[:, j : j + 1] * scale
        pivot = two[:, j + 1 : j + 2] - two[:, j : j + 1] * step
        lower = jnp.where(row > j + 1, left * scale + (right - left * step) * (two_cleared / pivot), 0.0)
        work = jnp.where(row == j + 1, two_cleared, work - lower)
    diagonal = jnp.sum(jnp.where(lane == row, work, 0.0), axis=1, keepdims=True)
    work = work / jnp.sqrt(diagonal)
    factor_ref[...] = jnp.where(lane >= row, work, 0.0)[:, :order]
    inverse_ref[...] = jnp.where(lane <= row, pltpu.roll(work, 128 - order, axis=1), 0.0)[:, :order]


def factor_and_inverse(parts, order, rows_all):
    square = jax.ShapeDtypeStruct((order, order), jnp.float32)
    return pl.pallas_call(
        functools.partial(factor_kernel, rows_all=rows_all),
        out_shape=(square, square),
        name="factor",
    )(parts)


def shape_of(*dims):
    return jax.ShapeDtypeStruct(dims, jnp.float32)


def shifted(block, axis, step):
    size = lax.axis_size(axis)
    return lax.ppermute(
        block, axis, [(i, i + step) for i in range(size) if 0 <= i + step < size]
    )


def steps_call(viscosity, local, *received):
    planes, length, columns = local[0].shape
    rows = length + 2 * WIDTH + 8
    return pl.pallas_call(
        steps_kernel,
        in_specs=[pl.BlockSpec(memory_space=pltpu.SMEM)] + whole(10),
        out_specs=whole(1)[0],
        out_shape=shape_of(planes, length, columns),
        scratch_shapes=[
            pltpu.VMEM((planes, rows, columns), jnp.float32),
            pltpu.VMEM((planes, rows, columns), jnp.float32),
            pltpu.VMEM((2, received[2].shape[0], rows, columns), jnp.float32),
            pltpu.VMEM((2, planes // PER, rows, columns), jnp.float32),
            pltpu.VMEM((3, WEIGHTS, rows, columns), jnp.float32),
            pltpu.VMEM((4 * V, rows, columns), jnp.float32),
            pltpu.VMEM((planes, rows, columns), jnp.float32),
            pltpu.VMEM((planes, rows, columns), jnp.float32),
            pltpu.VMEM((SPLIT * columns, 2 * columns), jnp.bfloat16),
        ],
        compiler_params=pltpu.CompilerParams(vmem_limit_bytes=VMEM_LIMIT),
        name="steps",
    )(viscosity, *local, *received)


def per_device(forcing, vel_axial, vel_radial, coupling, viscosity):
    vectors, variables, length, columns = forcing.shape
    planes = vectors * variables
    field = forcing.reshape(planes, length, columns)
    local = (field, coupling.reshape(V * V, length, columns), vel_axial, vel_radial)
    params = pltpu.CompilerParams(vmem_limit_bytes=VMEM_LIMIT)

    strip = shape_of((planes + PLANES) * WIDTH, columns)
    up, down = pl.pallas_call(
        pack_axial_kernel,
        in_specs=whole(4),
        out_specs=whole(2),
        out_shape=(strip, strip),
        compiler_params=params,
        name="pack_axial",
    )(*local)
    low = shifted(up, "ax", 1)
    high = shifted(down, "ax", -1)

    rim = shape_of(planes // PER + -(-PLANES // PER), length, columns)
    to_right, to_left = pl.pallas_call(
        pack_radial_kernel,
        in_specs=whole(4),
        out_specs=whole(2),
        out_shape=(rim, rim),
        compiler_params=params,
        name="pack_radial",
    )(*local)
    left = shifted(to_right, "rad", 1)
    right = shifted(to_left, "rad", -1)

    corner = shape_of(2 * rim.shape[0] * WIDTH, columns)
    rim_up, rim_down = pl.pallas_call(
        pack_corner_kernel,
        in_specs=whole(2),
        out_specs=whole(2),
        out_shape=(corner, corner),
        compiler_params=params,
        name="pack_corner",
    )(left, right)
    rim_low = shifted(rim_up, "ax", 1)
    rim_high = shifted(rim_down, "ax", -1)
    response = steps_call(viscosity, local, low, high, left, right, rim_low, rim_high)

    flattened = response.reshape(vectors, variables * length * columns)
    devices = lax.axis_size("ax") * lax.axis_size("rad")
    rows_all = variables * length * columns * devices
    local_gram = jnp.dot(flattened, flattened.T, precision=lax.Precision.HIGHEST)
    packed = jnp.concatenate([local_gram[8 * i : 8 * i + 8] for i in range(4)], axis=1)
    pairs = [(i, i ^ 1) for i in range(lax.axis_size("rad"))]
    packed = packed + lax.ppermute(packed, "rad", pairs)
    copies = jnp.broadcast_to(packed, (devices // 2, 8, 128))
    halves = [list(range(parity, devices, 2)) for parity in range(2)]
    parts = lax.all_to_all(copies, ("ax", "rad"), 0, 0, axis_index_groups=halves)
    upper_factor, lower_inverse = factor_and_inverse(parts, vectors, rows_all)
    basis = jnp.dot(lower_inverse, flattened, precision=lax.Precision.HIGHEST).reshape(forcing.shape)
    return (basis, upper_factor)


def solution(mesh):
    return jax.shard_map(
        per_device,
        mesh=mesh,
        in_specs=(
            P(None, None, "ax", "rad"),
            P("ax", "rad"),
            P("ax", "rad"),
            P(None, None, "ax", "rad"),
            P(),
        ),
        out_specs=(P(None, None, "ax", "rad"), P()),
        check_vma=False,
    )
```

```python
import functools

import jax
import jax.numpy as jnp
from jax import lax
from jax.experimental import pallas as pl
from jax.experimental.pallas import tpu as pltpu
from jax.sharding import PartitionSpec as P

STEPS = 3
TIME_STEP = 0.8
SECTIONS = 2 * STEPS
WIDTH = 2 * SECTIONS
V = 5
GROUP = 16
PER = 128 // GROUP
PLANES = V * V + 3
WEIGHTS = V * (V + 8)
VMEM_LIMIT = 56 << 20


def whole(count):
    return [pl.BlockSpec(memory_space=pltpu.VMEM) for _ in range(count)]


def lanes_of(shape):
    return lax.broadcasted_iota(jnp.int32, shape, 1)


def pack_axial_kernel(field_ref, coupling_ref, axial_ref, radial_ref, up_ref, down_ref):
    planes, length, _ = field_ref.shape
    low = length - WIDTH

    def put(slot, read):
        base = slot * WIDTH
        for start in range(0, WIDTH, 8):
            size = min(8, WIDTH - start)
            up_ref[pl.ds(base + start, size), :] = read(low + start, size)
            down_ref[pl.ds(base + start, size), :] = read(start, size)

    @pl.loop(0, planes // 8)
    def _(block):
        for inner in range(8):
            plane = block * 8 + inner
            put(plane, lambda start, size: field_ref[plane, pl.ds(start, size), :])

    for plane in range(V * V):
        put(planes + plane, lambda start, size: coupling_ref[plane, pl.ds(start, size), :])
    put(planes + V * V, lambda start, size: axial_ref[pl.ds(start, size), :])
    put(planes + V * V + 1, lambda start, size: radial_ref[pl.ds(start, size), :])
    put(planes + V * V + 2, lambda start, size: jnp.ones((size, 128), jnp.float32))


def chunks(length):
    rim = sorted({*range(0, WIDTH - 7, 8), WIDTH - 8})
    return (
        [(0, row, row) for row in rim]
        + [(1, row, WIDTH + row) for row in range(0, length, 8)]
        + [(2, row, WIDTH + length + row) for row in rim]
    )


def coefficient(plane, source, row, planes, coupling_ref, axial_ref, radial_ref, low_ref, high_ref):
    if source != 1:
        ref = low_ref if source == 0 else high_ref
        return ref[pl.ds((planes + plane) * WIDTH + row, 8), :]
    if plane < V * V:
        return coupling_ref[plane, pl.ds(row, 8), :]
    if plane == V * V + 2:
        return jnp.ones((8, 128), jnp.float32)
    return (axial_ref if plane == V * V else radial_ref)[pl.ds(row, 8), :]


def pack_radial_kernel(field_ref, coupling_ref, axial_ref, radial_ref, right_ref, left_ref):
    planes, length, _ = field_ref.shape
    groups = planes // (V * PER)
    lane = lanes_of((8, 128))

    def merge(tiles, offset):
        merged = pltpu.roll(tiles[0], offset, axis=1)
        for j in range(1, len(tiles)):
            merged = jnp.where(
                lane >= GROUP * j, pltpu.roll(tiles[j], (GROUP * j + offset) % 128, axis=1), merged
            )
        return merged

    def put(slot, row, tiles):
        right_ref[slot, pl.ds(row, 8), :] = merge(tiles, WIDTH)
        left_ref[slot, pl.ds(row, 8), :] = merge(tiles, 2)

    @pl.loop(0, groups)
    def _(group):
        for v in range(V):
            for row in range(0, length, 8):
                put(
                    group * V + v,
                    row,
                    [field_ref[(group * PER + j) * V + v, pl.ds(row, 8), :] for j in range(PER)],
                )

    for slot in range(-(-PLANES // PER)):
        for row in range(0, length, 8):
            tiles = [
                coefficient(plane, 1, row, planes, coupling_ref, axial_ref, radial_ref, None, None)
                for plane in range(slot * PER, min(PLANES, (slot + 1) * PER))
            ]
            put(groups * V + slot, row, tiles)


def pack_corner_kernel(left_ref, right_ref, up_ref, down_ref):
    slots, length, _ = left_ref.shape
    low = length - WIDTH
    for side, ref in ((0, left_ref), (1, right_ref)):
        for slot in range(slots):
            base = (side * slots + slot) * WIDTH
            for start in range(0, WIDTH, 8):
                size = min(8, WIDTH - start)
                up_ref[base + start : base + start + size, :] = ref[
                    slot, low + start : low + start + size, :
                ]
                down_ref[base + start : base + start + size, :] = ref[slot, start : start + size, :]


def neighbours(spread, speed):
    return (
        16.0 * spread + 8.0 * speed,
        16.0 * spread - 8.0 * speed,
        -spread - speed,
        speed - spread,
    )


def weights_of(raw, viscosity):
    axial = raw[V * V] * (-TIME_STEP / 12.0)
    radial = raw[V * V + 1] * (-TIME_STEP / 12.0)
    inside = raw[V * V + 2]
    found = []
    for v in range(V):
        spread = inside * (viscosity[v] * (TIME_STEP / 12.0))
        for w in range(V):
            value = raw[v * V + w] * TIME_STEP
            found.append(value + (1.0 - 60.0 * spread) if v == w else value)
        for speed in (axial, radial):
            found.extend(neighbours(spread, speed))
    return found


def steps_kernel(
    viscosity_ref,
    field_ref,
    coupling_ref,
    axial_ref,
    radial_ref,
    low_ref,
    high_ref,
    left_ref,
    right_ref,
    rim_low_ref,
    rim_high_ref,
    out_ref,
    now_ref,
    middle_ref,
    now_rim_ref,
    middle_rim_ref,
    weight_ref,
    edge_ref,
    first_ref,
    second_ref,
    band_ref,
):
    planes, length, _ = field_ref.shape
    vectors = planes // V
    groups = vectors // PER
    slots = groups * V
    extended = length + 2 * WIDTH
    lane = lanes_of((8, 128))
    place = lane % GROUP
    viscosity = [viscosity_ref[v] for v in range(V)]

    def spread_out(tile):
        reach = GROUP
        while reach < 128:
            tile = tile + pltpu.roll(tile, reach, axis=1)
            reach *= 2
        return tile

    shape = (128, 256)
    offset = lax.broadcasted_iota(jnp.int32, shape, 0) - lax.broadcasted_iota(
        jnp.int32, shape, 1
    )
    offset_column = lax.broadcasted_iota(jnp.int32, shape, 1)
    band = jnp.zeros(shape, jnp.float32)
    for gap, odd_part, even_part in ((1, 8.0, 16.0), (-1, -8.0, 16.0), (2, -1.0, -1.0), (-2, 1.0, -1.0)):
        band = jnp.where((offset == gap) & (offset_column < 128), odd_part, band)
        band = jnp.where((offset + 128 == gap) & (offset_column >= 128), even_part, band)
    for part in range(SPLIT):
        band_ref[pl.ds(128 * part, 128), :] = band.astype(jnp.bfloat16)

    @pl.loop(0, planes // 8)
    def _(block):
        for inner in range(8):
            plane = block * 8 + inner
            for source, row, target in chunks(length):
                if source == 1:
                    value = field_ref[plane, pl.ds(row, 8), :]
                else:
                    ref = low_ref if source == 0 else high_ref
                    value = ref[pl.ds(plane * WIDTH + row, 8), :]
                now_ref[plane, pl.ds(target, 8), :] = value

    packed = left_ref.shape[0]
    for side, own_ref in ((0, left_ref), (1, right_ref)):

        @pl.loop(0, packed)
        def _(slot):
            for source, row, target in chunks(length):
                if source == 1:
                    value = own_ref[slot, pl.ds(row, 8), :]
                else:
                    ref = rim_low_ref if source == 0 else rim_high_ref
                    value = ref[pl.ds((side * packed + slot) * WIDTH + row, 8), :]
                now_rim_ref[side, slot, pl.ds(target, 8), :] = value

    for source, row, target in chunks(length):
        raw = [
            coefficient(
                plane, source, row, planes, coupling_ref, axial_ref, radial_ref, low_ref, high_ref
            )
            for plane in range(PLANES)
        ]
        for index, value in enumerate(weights_of(raw, viscosity)):
            if index % (V + 8) < V + 4:
                weight_ref[0, index, pl.ds(target, 8), :] = value
        near = (lane >= WIDTH - 2) & (lane < WIDTH + 2)
        edge_speed, edge_inside = [
            spread_out(jnp.where(near, pltpu.roll(raw[plane], WIDTH, axis=1), 0.0))
            for plane in (V * V + 1, V * V + 2)
        ]
        edge_speed = edge_speed * (-TIME_STEP / 12.0)
        keeps = (
            place == WIDTH - 1,
            place == WIDTH,
            (place == WIDTH - 2) | (place == WIDTH - 1),
            (place == WIDTH) | (place == WIDTH + 1),
        )
        for v in range(V):
            spread = edge_inside * (viscosity[v] * (TIME_STEP / 12.0))
            for kind, value in enumerate(neighbours(spread, edge_speed)):
                edge_ref[v * 4 + kind, pl.ds(target, 8), :] = jnp.where(keeps[kind], value, 0.0)
        radial = raw[V * V + 1] * (-TIME_STEP / 12.0)
        weight_ref[0, V + 4, pl.ds(target, 8), :] = radial
        for v in range(V):
            weight_ref[0, v * (V + 8) + V + 5, pl.ds(target, 8), :] = raw[V * V + 2] * (
                viscosity[v] * (TIME_STEP / 12.0)
            )

    @pl.loop(0, extended // 8)
    def _(block):
        start = pl.multiple_of(block * 8, 8)
        for side in range(2):
            raw = []
            for plane in range(PLANES):
                tile = now_rim_ref[side, slots + plane // PER, pl.ds(start, 8), :]
                tile = pltpu.roll(tile, (128 - GROUP * (plane % PER)) % 128, axis=1)
                raw.append(spread_out(jnp.where(lane < GROUP, tile, 0.0)))
            for index, value in enumerate(weights_of(raw, viscosity)):
                weight_ref[1 + side, index, pl.ds(start, 8), :] = value

    def euler(v, kind, start, count, centers, vertical, sideways):
        def weight(index):
            return weight_ref[kind, v * (V + 8) + index, pl.ds(start, 8), :]

        totals = None
        for w in range(V):
            factor = weight(w)
            terms = [factor * centers[i][w] for i in range(count)]
            totals = terms if totals is None else [a + b for a, b in zip(totals, terms)]
        for index, step in enumerate((1, -1, 2, -2)):
            factor = weight(V + index)
            totals = [totals[i] + factor * vertical(i, step) for i in range(count)]
        if kind > 0:
            for index, step in enumerate((1, -1, 2, -2)):
                factor = weight(V + 4 + index)
                totals = [totals[i] + factor * sideways(i, step) for i in range(count)]
            return totals
        speed, spread = weight_ref[0, V + 4, pl.ds(start, 8), :], weight(V + 5)
        for i in range(count):
            one, two, rim = sideways(i, 0)
            totals[i] = ((totals[i] + rim) + speed * one) + spread * two
        return totals

    for section in range(1, SECTIONS + 1):
        odd = section % 2 == 1
        last = section == SECTIONS
        source, source_rim = (now_ref, now_rim_ref) if odd else (middle_ref, middle_rim_ref)
        target, target_rim = (middle_ref, middle_rim_ref) if odd else (now_ref, now_rim_ref)
        first = 2 * section
        blocks = -(-(extended - 2 * first) // 8)
        low_row, high_row = first // 8 * 8, -(-(extended - first) // 8) * 8

        @pl.loop(0, planes // BATCH)
        def _(batch):
            here = pl.ds(batch * BATCH, BATCH)
            rest = source[here, low_row:high_row, :].reshape(BATCH * (high_row - low_row), 128)
            halves = []
            for part in range(SPLIT):
                halves.append(rest.astype(jnp.bfloat16))
                if part < SPLIT - 1:
                    rest = rest - halves[-1].astype(jnp.float32)
            both = jnp.dot(
                jnp.concatenate(halves, axis=1), band_ref[...], preferred_element_type=jnp.float32
            )
            first_ref[here, low_row:high_row, :] = both[:, :128].reshape(BATCH, -1, 128)
            second_ref[here, low_row:high_row, :] = both[:, 128:].reshape(BATCH, -1, 128)

        @pl.loop(0, groups * blocks)
        def _(index):
            group, block = index // blocks, index % blocks
            start = first + block * 8
            joints = []
            for v in range(V):
                slot = group * V + v
                own = None
                for j in range(PER):
                    tile = source[(group * PER + j) * V + v, pl.ds(start, 8), :]
                    tile = pltpu.roll(tile, (GROUP * j + WIDTH) % 128, axis=1)
                    own = tile if own is None else jnp.where(lane >= GROUP * j, tile, own)
                left = source_rim[0, slot, pl.ds(start, 8), :]
                right = source_rim[1, slot, pl.ds(start, 8), :]
                inner = (place == WIDTH) | (place == WIDTH + 1)
                joint = jnp.where(inner, pltpu.roll(right, WIDTH - 2, axis=1), left)
                joints.append(
                    sum(
                        edge_ref[v * 4 + index, pl.ds(start, 8), :]
                        * pltpu.roll(joint, (128 - step) % 128, axis=1)
                        for index, step in enumerate((1, -1, 2, -2))
                    )
                )
                if not last:
                    source_rim[0, slot, pl.ds(start, 8), :] = jnp.where(inner, own, left)
                    source_rim[1, slot, pl.ds(start, 8), :] = jnp.where(
                        place < 2, pltpu.roll(own, 128 - (WIDTH - 2), axis=1), right
                    )

            if not last:
                for side in range(2):
                    slot = group * V
                    centers = [
                        [source_rim[side, slot + w, pl.ds(start, 8), :] for w in range(V)]
                    ]
                    for v in range(V):
                        (value,) = euler(
                            v,
                            1 + side,
                            start,
                            1,
                            centers,
                            lambda i, step: source_rim[side, slot + v, pl.ds(start + step, 8), :],
                            lambda i, step: pltpu.roll(centers[0][v], (128 - step) % 128, axis=1),
                        )
                        if not odd:
                            value = 0.5 * (value + target_rim[side, slot + v, pl.ds(start, 8), :])
                        target_rim[side, slot + v, pl.ds(start, 8), :] = value

            for part in range(PER // TOGETHER):
                bases = [(group * PER + part * TOGETHER + i) * V for i in range(TOGETHER)]
                centers = [
                    [source[base + w, pl.ds(start, 8), :] for w in range(V)] for base in bases
                ]
                for v in range(V):
                    rims = [
                        pltpu.roll(
                            joints[v],
                            (256 - WIDTH - GROUP * (part * TOGETHER + i)) % 128,
                            axis=1,
                        )
                        for i in range(TOGETHER)
                    ]
                    edge = (lane < 2) | (lane >= 126)

                    def sideways(i, step):
                        plane = bases[i] + v
                        return (
                            first_ref[plane, pl.ds(start, 8), :],
                            second_ref[plane, pl.ds(start, 8), :],
                            jnp.where(edge, rims[i], 0.0),
                        )

                    values = euler(
                        v,
                        0,
                        start,
                        TOGETHER,
                        centers,
                        lambda i, step: source[bases[i] + v, pl.ds(start + step, 8), :],
                        sideways,
                    )
                    for i in range(TOGETHER):
                        value = values[i]
                        if not odd:
                            value = 0.5 * (value + target[bases[i] + v, pl.ds(start, 8), :])
                        if last:
                            out_ref[bases[i] + v, pl.ds(start - WIDTH, 8), :] = value
                        else:
                            target[bases[i] + v, pl.ds(start, 8), :] = value


TOGETHER = 8
SPLIT = 2
BATCH = 80


def factor_kernel(parts_ref, factor_ref, inverse_ref, *, rows_all):
    total = jnp.sum(parts_ref[...], axis=0) * (1.0 / rows_all)
    order = factor_ref.shape[0]
    lane = lax.broadcasted_iota(jnp.int32, (order, 128), 1)
    row = lax.broadcasted_iota(jnp.int32, (order, 128), 0)
    pieces = [total] + [pltpu.roll(total, 128 - 32 * i, axis=1) for i in range(1, 4)]
    work = jnp.concatenate(pieces, axis=0)
    work = jnp.where(lane < order, work, jnp.where(lane == row + order, 1.0, 0.0))
    for j in range(order - 1):
        pivot_row = work[j : j + 1, :]
        scale = pivot_row / pivot_row[:, j : j + 1]
        column = jnp.where(row > j, jnp.broadcast_to(work[:, j : j + 1], work.shape), 0.0)
        work = work - column * scale
    diagonal = jnp.sum(jnp.where(lane == row, work, 0.0), axis=1, keepdims=True)
    work = work / jnp.sqrt(diagonal)
    factor_ref[...] = jnp.where(lane >= row, work, 0.0)[:, :order]
    inverse_ref[...] = jnp.where(lane <= row, pltpu.roll(work, 128 - order, axis=1), 0.0)[:, :order]


def factor_and_inverse(parts, order, rows_all):
    square = jax.ShapeDtypeStruct((order, order), jnp.float32)
    return pl.pallas_call(
        functools.partial(factor_kernel, rows_all=rows_all),
        out_shape=(square, square),
        name="factor",
    )(parts)


def shape_of(*dims):
    return jax.ShapeDtypeStruct(dims, jnp.float32)


def shifted(block, axis, step):
    size = lax.axis_size(axis)
    return lax.ppermute(
        block, axis, [(i, i + step) for i in range(size) if 0 <= i + step < size]
    )


def steps_call(viscosity, local, *received):
    planes, length, columns = local[0].shape
    rows = length + 2 * WIDTH + 8
    return pl.pallas_call(
        steps_kernel,
        in_specs=[pl.BlockSpec(memory_space=pltpu.SMEM)] + whole(10),
        out_specs=whole(1)[0],
        out_shape=shape_of(planes, length, columns),
        scratch_shapes=[
            pltpu.VMEM((planes, rows, columns), jnp.float32),
            pltpu.VMEM((planes, rows, columns), jnp.float32),
            pltpu.VMEM((2, received[2].shape[0], rows, columns), jnp.float32),
            pltpu.VMEM((2, planes // PER, rows, columns), jnp.float32),
            pltpu.VMEM((3, WEIGHTS, rows, columns), jnp.float32),
            pltpu.VMEM((4 * V, rows, columns), jnp.float32),
            pltpu.VMEM((planes, rows, columns), jnp.float32),
            pltpu.VMEM((planes, rows, columns), jnp.float32),
            pltpu.VMEM((SPLIT * columns, 2 * columns), jnp.bfloat16),
        ],
        compiler_params=pltpu.CompilerParams(vmem_limit_bytes=VMEM_LIMIT),
        name="steps",
    )(viscosity, *local, *received)


def per_device(forcing, vel_axial, vel_radial, coupling, viscosity):
    vectors, variables, length, columns = forcing.shape
    planes = vectors * variables
    field = forcing.reshape(planes, length, columns)
    local = (field, coupling.reshape(V * V, length, columns), vel_axial, vel_radial)
    params = pltpu.CompilerParams(vmem_limit_bytes=VMEM_LIMIT)

    strip = shape_of((planes + PLANES) * WIDTH, columns)
    up, down = pl.pallas_call(
        pack_axial_kernel,
        in_specs=whole(4),
        out_specs=whole(2),
        out_shape=(strip, strip),
        compiler_params=params,
        name="pack_axial",
    )(*local)
    low = shifted(up, "ax", 1)
    high = shifted(down, "ax", -1)

    rim = shape_of(planes // PER + -(-PLANES // PER), length, columns)
    to_right, to_left = pl.pallas_call(
        pack_radial_kernel,
        in_specs=whole(4),
        out_specs=whole(2),
        out_shape=(rim, rim),
        compiler_params=params,
        name="pack_radial",
    )(*local)
    left = shifted(to_right, "rad", 1)
    right = shifted(to_left, "rad", -1)

    corner = shape_of(2 * rim.shape[0] * WIDTH, columns)
    rim_up, rim_down = pl.pallas_call(
        pack_corner_kernel,
        in_specs=whole(2),
        out_specs=whole(2),
        out_shape=(corner, corner),
        compiler_params=params,
        name="pack_corner",
    )(left, right)
    rim_low = shifted(rim_up, "ax", 1)
    rim_high = shifted(rim_down, "ax", -1)
    response = steps_call(viscosity, local, low, high, left, right, rim_low, rim_high)

    flattened = response.reshape(vectors, variables * length * columns)
    devices = lax.axis_size("ax") * lax.axis_size("rad")
    rows_all = variables * length * columns * devices
    local_gram = jnp.dot(flattened, flattened.T, precision=lax.Precision.HIGHEST)
    packed = jnp.concatenate([local_gram[8 * i : 8 * i + 8] for i in range(4)], axis=1)
    for gap in (1, 2):
        pairs = [(i, i ^ gap) for i in range(lax.axis_size("rad"))]
        packed = packed + lax.ppermute(packed, "rad", pairs)
    copies = jnp.broadcast_to(packed, (devices // 4, 8, 128))
    quarters = [list(range(first, devices, 4)) for first in range(4)]
    parts = lax.all_to_all(copies, ("ax", "rad"), 0, 0, axis_index_groups=quarters)
    upper_factor, lower_inverse = factor_and_inverse(parts, vectors, rows_all)
    basis = jnp.dot(lower_inverse, flattened, precision=lax.Precision.HIGHEST).reshape(forcing.shape)
    return (basis, upper_factor)


def solution(mesh):
    return jax.shard_map(
        per_device,
        mesh=mesh,
        in_specs=(
            P(None, None, "ax", "rad"),
            P("ax", "rad"),
            P("ax", "rad"),
            P(None, None, "ax", "rad"),
            P(),
        ),
        out_specs=(P(None, None, "ax", "rad"), P()),
        check_vma=False,
    )
```
